128 devices in a mesh: gx: 8 (over y, core), gy: 16 (over z, x).
Axes of the slice: x: 4, y: 4, z: 4, core: 2. Of those that a mesh axis runs over, the one named last changes fastest.
Arguments:
- elem_volume: float32 [294912], P(('gx', 'gy')), may hold values from 0.5 to 1.5
- elem_velocity: float32 [3, 294912], P(None, ('gx', 'gy')), may hold values from -6 to 6
- elem_energy: float32 [294912], P(('gx', 'gy')), may hold values from 0.3 to 3
- elem_mat: int32 [294912], P(('gx', 'gy')), may hold values from 0 to 7
- elem_dest: int32 [2304], P(('gx', 'gy')), may hold values from 0 to 127, as said below
- tile_slot: int32 [16384], P(('gx', 'gy')), may hold values from 0 to 255, as said below
- tile_cell: int32 [16384], P(('gx', 'gy')), may hold values from 0 to 1023
- tile_weight: bfloat16 [16384, 128, 128], P(('gx', 'gy')), may hold values from 0.00390625 to 0.01171875
- tile_count: int32 [128], P(('gx', 'gy')), may hold values from 32 to 128, as said below
- cell_state: float32 [12, 512, 32768], P(None, 'gx', 'gy'), may hold values from -4 to 4, as said below
- mat_props: float32 [2, 8], replicated, may hold values from 0.5 to 4
Outputs:
- remapped: float32 [12, 512, 32768], P(None, 'gx', 'gy')
- elem_pressure: bfloat16 [294912], P(('gx', 'gy'))
The draws below stay inside these ranges and needn't reach their ends.
Inputs may be any that keep to these rules, and one draw needn't show every extreme that they name: `elem_dest`: each device sends exactly 2 of its blocks to each of the nine devices at offsets -1, 0, +1 along gx and along gy, wrapping at the ends, itself included. `tile_slot`: A value is source * 2 + rank of a block that was sent to this device; every block sent to a device is named by some tile below its count. `tile_count`: some device has all 128 tiles counted. `cell_state`: the volume and energy rows lie between 0.1 and 1; the three momentum rows are signed.
All inputs are finite; a program needn't handle non-finite values.
Results may differ from the reference program's by a relative error of at most 0.0024.
Values may be sent and summed in bfloat16 or wider, within the bound.
A program may use at most 192 MiB of HBM per device.

```python
import math
import jax
import jax.numpy as jnp
from jax import lax

MAT = 8
P_SIZE = 12
NZ = 64
BLK = 128
NXD = 64
NYD = 32
CAP = 2
TCAP = 128
GRID_X = 8
GRID_Y = 16
EB_DEV = 18
EBLOCKS = 2304
ELEMS = 294912
NX = 512
NY = 512
CB_DEV = 1024
TILES = 16384
LOW = 32


def neighbour_index(pos_x, pos_y, which, sign):
    step_x = which // 3 - 1
    step_y = which % 3 - 1
    return (pos_x + sign * step_x) % GRID_X * GRID_Y + (pos_y + sign * step_y) % GRID_Y


def draw_elem_dest(key, part):
    nodes = GRID_X * GRID_Y
    keys = jax.random.split(key, nodes)

    def single(sub, device):
        order = jax.random.permutation(sub, EB_DEV)
        return neighbour_index(device // GRID_Y, device % GRID_Y, order // CAP, 1)
    return jax.vmap(single)(keys, jnp.arange(nodes, dtype=jnp.int32)).reshape(-1).astype(jnp.int32)


def draw_tile_slot(key, part):
    nodes = GRID_X * GRID_Y
    keys = jax.random.split(key, nodes)

    def single(sub, device):
        first, second, third = jax.random.split(sub, 3)
        places = jnp.arange(TCAP, dtype=jnp.int32)
        extra_which = jax.random.randint(first, (TCAP,), 0, 9)
        extra_rank = jax.random.randint(second, (TCAP,), 0, CAP)
        which = jnp.where(places < 9 * CAP, places // CAP, extra_which)
        rank = jnp.where(places < 9 * CAP, places % CAP, extra_rank)
        source = neighbour_index(device // GRID_Y, device % GRID_Y, which, -1)
        slots = source * CAP + rank
        head = jax.random.permutation(third, slots[:LOW])
        return jnp.concatenate([head, slots[LOW:]])
    return jax.vmap(single)(keys, jnp.arange(nodes, dtype=jnp.int32)).reshape(-1).astype(jnp.int32)


def draw_tile_count(key, part):
    nodes = GRID_X * GRID_Y
    first, second = jax.random.split(key)
    counts = jax.random.randint(first, (nodes,), LOW, TCAP + 1)
    busiest = jax.random.randint(second, (), 0, nodes)
    return jnp.where(jnp.arange(nodes) == busiest, TCAP, counts).astype(jnp.int32)


def draw_cell_state(key, part):
    count = MAT + 4
    fresh_key = jax.random.fold_in(key, 17)
    unit = jax.random.uniform(fresh_key, (count, NX, NY * NZ), jnp.float32)
    quantity = jnp.arange(count, dtype=jnp.int32)
    moving = (quantity >= MAT) & (quantity < MAT + 3)
    level = 0.1 + 0.9 * unit
    drift = -4.0 + 8.0 * unit
    return jnp.where(moving[:, None, None], drift, level).astype(jnp.float32)


def plant(values, rng, low, largest):
    longest = values.shape.index(max(values.shape))
    spots = []
    for shift in (0, 1):
        where = [jax.random.randint(jax.random.fold_in(rng, axis), (), 0, length) for axis, length in enumerate(values.shape)]
        where[longest] = (where[longest] + shift) % values.shape[longest]
        spots.append(tuple(where))
    return values.at[spots[0]].set(low).at[spots[1]].set(largest)


def shard_levels(rng, dims, cuts, least, top_value):
    level = 1.0
    for dim, shards_of in cuts:
        draws = jax.random.uniform(jax.random.fold_in(jax.random.fold_in(rng, 6), dim), (shards_of,), jnp.float32, least / len(cuts), top_value / len(cuts))
        level = level * jnp.repeat(jnp.exp(draws), dims[dim] // shards_of).reshape((-1,) + (1,) * (len(dims) - 1 - dim))
    return level


def noise(rng, shape, scale, bound, cuts=(), held_as=jnp.bfloat16):
    array = jax.random.normal(rng, shape, jnp.float32) * scale
    if len(cuts) > 0:
        array = shard_levels(rng, shape, cuts, -0.22, 0.18) * array
    return jnp.clip(array, min=-bound, max=bound).astype(held_as)


def setup_inputs(seed: int = 0) -> dict:
    seeds = jax.random.split(jax.random.key(seed), 12)
    return {
        "elem_volume": jnp.clip(0.5 + 1.0 * jax.random.uniform(seeds[0], (ELEMS,), jnp.float32) ** shard_levels(seeds[0], (ELEMS,), ((0, 128),), -0.2, 0.2), 0.5, 1.5),
        "elem_velocity": noise(seeds[1], (3, ELEMS), 1.5, 6.0, ((1, 128),), jnp.float32),
        "elem_energy": jnp.clip(jnp.exp(math.log(3.0) - 2.3025851 * jax.random.uniform(seeds[2], (ELEMS,), jnp.float32) ** shard_levels(seeds[2], (ELEMS,), ((0, 128),), -0.2, 0.2)), 0.3, 3.0),
        "elem_mat": plant(jax.random.randint(seeds[3], (ELEMS,), 0, MAT), jax.random.fold_in(seeds[3], 1), 0, MAT - 1).astype(jnp.int32),
        "elem_dest": draw_elem_dest(jax.random.fold_in(seeds[11], 71), 0),
        "tile_slot": draw_tile_slot(jax.random.fold_in(seeds[11], 71), 0),
        "tile_cell": plant(jax.random.randint(seeds[6], (TILES,), 0, CB_DEV), jax.random.fold_in(seeds[6], 1), 0, CB_DEV - 1).astype(jnp.int32),
        "tile_weight": jnp.clip(0.00390625 + 0.0078125 * jax.random.uniform(seeds[7], (TILES, BLK, BLK), jnp.float32) ** shard_levels(seeds[7], (TILES, BLK, BLK), ((0, 128),), -0.2, 0.2), 0.00390625, 0.01171875).astype(jnp.bfloat16),
        "tile_count": draw_tile_count(jax.random.fold_in(seeds[11], 71), 0),
        "cell_state": draw_cell_state(jax.random.fold_in(seeds[11], 71), 0),
        "mat_props": jnp.clip(jnp.exp(jax.random.uniform(seeds[10], (2, MAT), jnp.float32, math.log(0.5), math.log(4.0))), 0.5, 4.0),
    }


time_step = 0.8


def face_flux(q_lo, q_hi, u_lo, u_hi):
    speed = 0.5 * (u_lo + u_hi)
    return 0.5 * (speed * (q_lo + q_hi) - jnp.abs(speed) * (q_hi - q_lo))


def reference(elem_volume, elem_velocity, elem_energy, elem_mat, elem_dest, tile_slot, tile_cell, tile_weight, tile_count, cell_state, mat_props):
    nodes = GRID_X * GRID_Y
    density = mat_props[0]
    modulus = mat_props[1]
    onehot = (elem_mat[None, :] == jnp.arange(MAT, dtype=jnp.int32)[:, None]).astype(jnp.float32)
    mass_e = elem_volume * jnp.sum(onehot * density[:, None], axis=0)
    rows = jnp.concatenate([onehot * elem_volume[None, :], mass_e[None, :] * elem_velocity, (mass_e * elem_energy)[None, :]], axis=0).astype(jnp.bfloat16)
    payload = rows.reshape(P_SIZE, EBLOCKS, BLK).transpose(1, 0, 2)

    dest_two = elem_dest.reshape(nodes, EB_DEV)
    index = jnp.arange(EB_DEV, dtype=jnp.int32)
    earlier = index[:, None] > index[None, :]
    same = dest_two[:, :, None] == dest_two[:, None, :]
    rank = jnp.sum((same & earlier[None]).astype(jnp.int32), axis=2)
    block_key = dest_two * (nodes * CAP) + jnp.arange(nodes, dtype=jnp.int32)[:, None] * CAP + rank
    block_key = block_key.reshape(-1)
    order = jnp.argsort(block_key).astype(jnp.int32)
    sorted_key = block_key[order]
    tile_key = jnp.repeat(jnp.arange(nodes, dtype=jnp.int32), TCAP) * (nodes * CAP) + tile_slot
    tile_block = order[jnp.searchsorted(sorted_key, tile_key)].astype(jnp.int32)

    valid = (jnp.arange(TCAP, dtype=jnp.int32)[None, :] < tile_count[:, None]).astype(jnp.float32)
    block_two = tile_block.reshape(nodes, TCAP)
    cell_two = tile_cell.reshape(nodes, TCAP)
    weight_two = tile_weight.reshape(nodes, TCAP, BLK, BLK)

    def deposit(item):
        blocks, cells, weights, flags = item
        picked = payload[blocks].astype(jnp.float32)
        contrib = jnp.einsum('trb,tbc->trc', picked, weights.astype(jnp.float32)) * flags[:, None, None]
        return jax.ops.segment_sum(contrib, cells, num_segments=CB_DEV)

    dep_all = lax.map(deposit, (block_two, cell_two, weight_two, valid))
    dep = dep_all.reshape(GRID_X, GRID_Y, CB_DEV, P_SIZE, BLK).transpose(3, 0, 1, 2, 4)
    dep = dep.reshape(P_SIZE, GRID_X, GRID_Y, NXD, NYD, NZ).transpose(0, 1, 3, 2, 4, 5).reshape(P_SIZE, NX, NY, NZ)

    q = cell_state.reshape(P_SIZE, NX, NY, NZ) + dep
    mass = 1.0 + jnp.sum(density[:, None, None, None] * q[:MAT], axis=0)
    u_x = q[MAT] / mass
    u_y = q[MAT + 1] / mass
    qx = jnp.pad(q, ((0, 0), (1, 1), (0, 0), (0, 0)))
    vx = jnp.pad(u_x, ((1, 1), (0, 0), (0, 0)))[None]
    flux_x = face_flux(qx[:, :-1], qx[:, 1:], vx[:, :-1], vx[:, 1:])
    qy = jnp.pad(q, ((0, 0), (0, 0), (1, 1), (0, 0)))
    vy = jnp.pad(u_y, ((0, 0), (1, 1), (0, 0)))[None]
    flux_y = face_flux(qy[:, :, :-1], qy[:, :, 1:], vy[:, :, :-1], vy[:, :, 1:])
    fresh = q - time_step * (flux_x[:, 1:] - flux_x[:, :-1] + flux_y[:, :, 1:] - flux_y[:, :, :-1])
    remapped = fresh.reshape(P_SIZE, NX, NY * NZ)

    volumes = fresh[:MAT]
    pressure = jnp.sum(modulus[:, None, None, None] * volumes * (1.0 + 0.5 * volumes), axis=0) + 0.4 * fresh[P_SIZE - 1]
    pressure = pressure.astype(jnp.bfloat16)
    press_dev = pressure.reshape(GRID_X, NXD, GRID_Y, NYD, NZ).transpose(0, 2, 1, 3, 4).reshape(nodes, CB_DEV, BLK)

    def sample(item):
        cells, weights, flags, press = item
        local = press[cells].astype(jnp.float32)
        wide = weights.astype(jnp.float32)
        numer = jnp.einsum('tec,tc->te', wide, local) * flags[:, None]
        denom = jnp.sum(wide, axis=2) * flags[:, None]
        return numer, denom

    numer, denom = lax.map(sample, (cell_two, weight_two, valid, press_dev))
    numer = jax.ops.segment_sum(numer.reshape(-1, BLK), tile_block, num_segments=EBLOCKS)
    denom = jax.ops.segment_sum(denom.reshape(-1, BLK), tile_block, num_segments=EBLOCKS)
    elem_pressure = (numer / jnp.maximum(denom, 1.0)).astype(jnp.bfloat16).reshape(ELEMS)
    return remapped, elem_pressure
```

```python
import functools

import jax
import jax.numpy as jnp
from jax import lax
from jax.experimental import pallas as pl
from jax.experimental.pallas import tpu as pltpu
from jax.sharding import PartitionSpec as P

MAT = 8
NQ = 12
NZ = 64
BLK = 128
CAP = 2
TIME_STEP = 0.8
NEAR = [(a, b) for a in range(3) for b in range(3)]
OWN = 4
F32 = jnp.float32
BF16 = jnp.bfloat16
MESH = pl.DeviceIdType.MESH


def kernel(
    dims,
    vol, vel, ene, mat, cell_v, dest_s, slot_s, cell_s, count_s, props_s, w_hbm, state_hbm,
    out_ref, eo_ref,
    wts, q_ref, f_ref, s_ref, c_ref, press, blk, outg, recv, xs, xr, ys, yr, anss, ret,
    w_sem, q_sem, o_sem, pay_s, pay_r, hx_s, hx_r, hy_s, hy_r, ret_s, ret_r,
):
    gx, gy, n_blk, n_tiles, wx, n_yb = dims
    px = lax.axis_index("gx")
    py = lax.axis_index("gy")
    group = 8
    n_chunk = 4
    tiles_chunk = n_tiles // n_chunk
    pad = 8
    row_x = pad + NQ * wx
    row_y = row_x + wx

    def dev(a, b, sign):
        return (lax.rem(px + sign * (a - 1) + gx, gx), lax.rem(py + sign * (b - 1) + gy, gy))

    def w_copy(i):
        part = pl.ds(i * tiles_chunk, tiles_chunk)
        return pltpu.make_async_copy(w_hbm.at[part], wts.at[part], w_sem.at[i])

    def q_copy(yb):
        return pltpu.make_async_copy(
            state_hbm.at[:, pl.ds(yb * BLK, BLK)],
            q_ref.at[yb + 1, pl.ds(pad, NQ * wx)],
            q_sem.at[yb],
        )

    def o_copy(yb):
        return pltpu.make_async_copy(
            f_ref.at[yb, pl.ds(0, NQ * wx)], out_ref.at[:, pl.ds(yb * BLK, BLK)], o_sem.at[yb]
        )

    ret[...] = jnp.zeros(ret.shape, F32)
    barrier = pltpu.get_barrier_semaphore()
    for a, b in NEAR:
        if (a, b) != (1, 1):
            pl.semaphore_signal(barrier, inc=1, device_id=dev(a, b, 1), device_id_type=MESH)
    for i in range(n_chunk):
        w_copy(i).start()
    for yb in range(n_yb):
        q_copy(yb).start()

    sub8 = lax.broadcasted_iota(jnp.int32, (8, BLK), 0)
    dens = [props_s[0, m] for m in range(MAT)]
    stiff = [props_s[1, m] for m in range(MAT)]
    dens_col = jnp.zeros((8, BLK), F32)
    for m in range(MAT):
        dens_col = jnp.where(sub8 == m, dens[m], dens_col)
    blk[...] = jnp.zeros(blk.shape, F32)
    for j in range(n_blk):
        hit = jnp.broadcast_to(mat[j : j + 1, :], (8, BLK)) == sub8
        v = vol[j : j + 1, :]
        blk[j, 0:8, :] = jnp.where(hit, jnp.broadcast_to(v, (8, BLK)), 0.0)
        mass = v * jnp.sum(jnp.where(hit, dens_col, 0.0), axis=0, keepdims=True)
        blk[j, 8:11, :] = mass * vel[:, j * BLK : (j + 1) * BLK]
        blk[j, 11:12, :] = mass * ene[j : j + 1, :]
    first, second = [], []
    keys = []
    for j in range(n_blk):
        d = dest_s[j]
        ka = lax.rem(d // gy - px + 1 + gx, gx)
        kb = lax.rem(lax.rem(d, gy) - py + 1 + gy, gy)
        keys.append(ka * 3 + kb)
    for n in range(9):
        low = jnp.int32(0)
        total = jnp.int32(0)
        for j in reversed(range(n_blk)):
            same = keys[j] == n
            low = jnp.where(same, jnp.int32(j), low)
            total = total + jnp.where(same, jnp.int32(j), jnp.int32(0))
        first.append(low)
        second.append(jnp.minimum(total - low, n_blk - 1))
    for n in range(9):
        for rank, src in ((0, first[n]), (1, second[n])):
            value = blk[src].astype(BF16)
            if n == OWN:
                recv[2 * n + rank] = value
            else:
                outg[2 * n + rank] = value

    pl.semaphore_wait(barrier, 8)
    pay = []
    for n, (a, b) in enumerate(NEAR):
        if n != OWN:
            i = len(pay)
            pay.append(
                pltpu.make_async_remote_copy(
                    src_ref=outg.at[pl.ds(2 * n, 2)], dst_ref=recv.at[pl.ds(2 * n, 2)],
                    send_sem=pay_s.at[i], recv_sem=pay_r.at[i],
                    device_id=dev(a, b, 1), device_id_type=MESH,
                )
            )
            pay[-1].start()

    rows_all = q_ref.shape[1]
    n_rows = 16 * wx

    def clear_end(i, carry):
        at = pl.multiple_of(i * 8, 8)
        q_ref[0, pl.ds(at, 8), :] = jnp.zeros((8, BLK), F32)
        q_ref[n_yb + 1, pl.ds(at, 8), :] = jnp.zeros((8, BLK), F32)
        return carry

    lax.fori_loop(0, rows_all // 8, clear_end, 0)

    def clear_tail(yb, carry):
        q_ref[yb + 1, 0:pad, :] = jnp.zeros((pad, BLK), F32)
        tail = rows_all - (row_y + wx)
        q_ref[yb + 1, row_y + wx : rows_all, :] = jnp.zeros((tail, BLK), F32)
        return carry

    lax.fori_loop(0, n_yb, clear_tail, 0)
    anss[...] = jnp.zeros(anss.shape, F32)

    for c in pay:
        c.wait_recv()
    for i in range(n_chunk):
        w_copy(i).wait()

    def local_slot(t):
        s = slot_s[t]
        source = s // CAP
        a = lax.rem(px - source // gy + 1 + gx, gx)
        b = lax.rem(py - lax.rem(source, gy) + 1 + gy, gy)
        return jnp.minimum((a * 3 + b) * CAP + lax.rem(s, CAP), n_blk - 1)

    def contrib(i, carry):
        for g in range(group):
            t = i * group + g
            c = jnp.dot(recv[local_slot(t)], wts[t], preferred_element_type=F32)
            s_ref[pl.ds(t, 16, stride=n_tiles), :] = c
        return carry

    lax.fori_loop(0, n_tiles // group, contrib, 0)

    def split(p, carry):
        for h in range(2):
            at = pl.multiple_of((2 * p + h) * n_tiles, n_tiles)
            value = s_ref[pl.ds(at, n_tiles), :]
            high = value.astype(BF16)
            c_ref[p, 0:n_tiles, h * BLK : (h + 1) * BLK] = high
            c_ref[p, n_tiles : 2 * n_tiles, h * BLK : (h + 1) * BLK] = (
                value - high.astype(F32)
            ).astype(BF16)
        return carry

    lax.fori_loop(0, NQ // 2, split, 0)

    lane_t = lax.broadcasted_iota(jnp.int32, (1, n_tiles), 1)
    cell_m = jnp.broadcast_to(jnp.where(lane_t < count_s[0], cell_v[...], -1), (wx, n_tiles))
    cell_at = lax.broadcasted_iota(jnp.int32, (wx, n_tiles), 0) * n_yb

    def deposit(yb):
        q_copy(yb).wait()
        pick = jnp.where(cell_m == cell_at + yb, 1.0, 0.0).astype(BF16)
        left = jnp.concatenate([pick, pick], axis=1)
        mass = jnp.ones((wx, BLK), F32)
        moving = []
        for p in range(NQ // 2):
            both = jnp.dot(left, c_ref[p], preferred_element_type=F32)
            for h in range(2):
                r = 2 * p + h
                rows = pl.ds(pad + r * wx, wx)
                value = q_ref[yb + 1, rows, :] + both[:, h * BLK : (h + 1) * BLK]
                q_ref[yb + 1, rows, :] = value
                if r < MAT:
                    mass = mass + dens[r] * value
                elif r < MAT + 2:
                    moving.append(value)
        q_ref[yb + 1, pl.ds(row_x, wx), :] = moving[0] / mass
        q_ref[yb + 1, pl.ds(row_y, wx), :] = moving[1] / mass

    def deposit_ends(i, carry):
        deposit(i * (n_yb - 1))
        return carry

    lax.fori_loop(0, 2, deposit_ends, 0)

    lane = lax.broadcasted_iota(jnp.int32, (wx, BLK), 1)
    upper = lane >= NZ

    def rows_of(r):
        return pl.ds(pad + r * wx, wx)

    def pair(yb, p, top):
        if p < NQ // 2:
            one, two = q_ref[yb + 1, rows_of(2 * p), :], q_ref[yb + 1, rows_of(2 * p + 1), :]
        else:
            one = q_ref[yb + 1, pl.ds(row_y, wx), :]
            two = one
        turned = pltpu.roll(one, NZ, axis=1)
        return jnp.where(upper, two, turned) if top else jnp.where(upper, turned, two)

    for p in range(NQ // 2 + 1):
        ys[0, p] = pair(0, p, False).astype(BF16)
        ys[1, p] = pair(n_yb - 1, p, True).astype(BF16)
    halo = []
    for e, b in ((0, 0), (1, 2)):
        halo.append(
            pltpu.make_async_remote_copy(
                src_ref=ys.at[e], dst_ref=yr.at[1 - e], send_sem=hy_s.at[e], recv_sem=hy_r.at[1 - e],
                device_id=dev(1, b, 1), device_id_type=MESH,
            )
        )
        halo[-1].start()

    def deposit_inner(i, carry):
        deposit(i)
        return carry

    lax.fori_loop(1, n_yb - 1, deposit_inner, 0)

    def pack_x(yb, carry):
        xs[0, yb] = q_ref[yb + 1, pl.ds(pad, 16, stride=wx), :].astype(BF16)
        xs[1, yb] = q_ref[yb + 1, pl.ds(pad + wx - 1, 16, stride=wx), :].astype(BF16)
        return carry

    lax.fori_loop(0, n_yb, pack_x, 0)
    for e, a in ((0, 0), (1, 2)):
        halo.append(
            pltpu.make_async_remote_copy(
                src_ref=xs.at[e], dst_ref=xr.at[1 - e], send_sem=hx_s.at[e], recv_sem=hx_r.at[1 - e],
                device_id=dev(a, 1, 1), device_id_type=MESH,
            )
        )
        halo[-1].start()

    half = wx // 2
    sub = lax.broadcasted_iota(jnp.int32, (half, BLK), 0)
    lane_h = lax.broadcasted_iota(jnp.int32, (half, BLK), 1)
    upper_h = lane_h >= NZ

    def remap(yb, carry):
        for part in range(2):
            x0 = part * half

            def at(base, shift=0):
                return pl.ds(base + x0 + shift, half)

            ux = q_ref[yb + 1, at(row_x), :]
            lo = 0.5 * (q_ref[yb + 1, at(row_x, -1), :] + ux)
            hi = 0.5 * (ux + q_ref[yb + 1, at(row_x, 1), :])
            if part == 0:
                lo = jnp.where(sub == 0, 0.0, lo)
            else:
                hi = jnp.where(sub == half - 1, 0.0, hi)
            uy = q_ref[yb + 1, at(row_y), :]
            prev, after = q_ref[yb, at(row_y), :], q_ref[yb + 2, at(row_y), :]
            y_hi = 0.5 * (uy + pltpu.roll(jnp.where(upper_h, uy, after), NZ, axis=1))
            y_lo = 0.5 * (uy + pltpu.roll(jnp.where(upper_h, prev, uy), NZ, axis=1))
            place = lane_h + yb * BLK
            y_lo = jnp.where(place < NZ, 0.0, y_lo)
            y_hi = jnp.where(place >= n_yb * BLK - NZ, 0.0, y_hi)
            c_xm = TIME_STEP * jnp.maximum(lo, 0.0)
            c_xp = -TIME_STEP * jnp.minimum(hi, 0.0)
            c_ym = TIME_STEP * jnp.maximum(y_lo, 0.0)
            c_yp = -TIME_STEP * jnp.minimum(y_hi, 0.0)
            c_0 = 1.0 - TIME_STEP * (
                (jnp.maximum(hi, 0.0) - jnp.minimum(lo, 0.0))
                + (jnp.maximum(y_hi, 0.0) - jnp.minimum(y_lo, 0.0))
            )
            t_p = pltpu.roll(c_yp, NZ, axis=1)
            t_m = pltpu.roll(c_ym, NZ, axis=1)
            own = jnp.where(upper_h, t_p, t_m)
            other = jnp.where(upper_h, t_m, t_p)
            acc = jnp.zeros((half, BLK), F32)
            for r in range(NQ):
                base = pad + r * wx
                q = q_ref[yb + 1, at(base), :]
                beside = jnp.where(upper_h, q_ref[yb, at(base), :], q_ref[yb + 2, at(base), :])
                fresh = (
                    c_0 * q
                    + c_xm * q_ref[yb + 1, at(base, -1), :]
                    + c_xp * q_ref[yb + 1, at(base, 1), :]
                    + pltpu.roll(own * q + other * beside, NZ, axis=1)
                )
                f_ref[yb, pl.ds(r * wx + x0, half), :] = fresh
                if r < MAT:
                    acc = acc + fresh * (stiff[r] + (0.5 * stiff[r]) * fresh)
                elif r == NQ - 1:
                    acc = acc + 0.4 * fresh
            press[pl.ds(pl.multiple_of(yb * wx + x0, half), half), :] = acc.astype(BF16).astype(F32)
        return carry

    lax.fori_loop(0, n_yb, remap, 0)

    for c in halo[:2]:
        c.wait_recv()
    has = [
        jnp.where(py > 0, 1.0, 0.0).astype(F32),
        jnp.where(py < gy - 1, 1.0, 0.0).astype(F32),
    ]
    for e, yb in ((0, 0), (1, n_yb - 1)):
        inside = jnp.logical_not(upper) if e == 0 else upper
        speed = 0.5 * (q_ref[yb + 1, pl.ds(row_y, wx), :] + has[e] * yr[e, NQ // 2].astype(F32))
        speed = jnp.where(inside, TIME_STEP * speed, 0.0)
        pos, neg = jnp.maximum(speed, 0.0), jnp.minimum(speed, 0.0)
        w_far, w_own = (has[e] * pos, neg) if e == 0 else (-has[e] * neg, -pos)
        acc = jnp.zeros((wx, BLK), F32)
        for p in range(NQ // 2):
            packed = yr[e, p].astype(F32)
            for h in range(2):
                r = 2 * p + h
                far = packed if h == 0 else pltpu.roll(packed, NZ, axis=1)
                rows = pl.ds(r * wx, wx)
                fresh = f_ref[yb, rows, :] + (w_far * far + w_own * q_ref[yb + 1, rows_of(r), :])
                f_ref[yb, rows, :] = fresh
                if r < MAT:
                    acc = acc + fresh * (stiff[r] + (0.5 * stiff[r]) * fresh)
                elif r == NQ - 1:
                    acc = acc + 0.4 * fresh
        press[yb * wx : (yb + 1) * wx, :] = acc.astype(BF16).astype(F32)

    for c in halo[2:]:
        c.wait_recv()
    sub16 = lax.broadcasted_iota(jnp.int32, (16, BLK), 0)
    lin = jnp.zeros((16, BLK), F32)
    for m in range(MAT):
        lin = jnp.where(sub16 == m, stiff[m], lin)
    quad = 0.5 * lin
    lin = jnp.where(sub16 == NQ - 1, 0.4, lin)
    has = [
        jnp.where(px > 0, 1.0, 0.0).astype(F32),
        jnp.where(px < gx - 1, 1.0, 0.0).astype(F32),
    ]

    def border_x(yb, carry):
        for e, x in ((0, 0), (1, wx - 1)):
            far = xr[e, yb].astype(F32) * has[e]
            q = q_ref[yb + 1, pl.ds(pad + x, 16, stride=wx), :]
            speed = (0.5 * TIME_STEP) * (q[NQ : NQ + 1] + far[NQ : NQ + 1])
            pos, neg = jnp.maximum(speed, 0.0), jnp.minimum(speed, 0.0)
            change = (pos * far + neg * q) if e == 0 else -(pos * q + neg * far)
            rows = pl.ds(x, 16, stride=wx)
            fresh = f_ref[yb, rows, :] + change
            f_ref[yb, rows, :] = fresh
            terms = jnp.where(sub16 < NQ, fresh * (lin + quad * fresh), 0.0)
            value = jnp.sum(terms, axis=0, keepdims=True)
            press[pl.ds(yb * wx + x, 1), :] = value.astype(BF16).astype(F32)
        o_copy(yb).start()
        return carry

    lax.fori_loop(0, n_yb, border_x, 0)

    sub48 = lax.broadcasted_iota(jnp.int32, (48, BLK), 0)
    count = count_s[0]

    def sample(i, acc):
        lefts, rights = [], []
        for g in range(group):
            t = i * group + g
            s = jnp.where(t < count, local_slot(t), jnp.int32(100))
            c = cell_s[t]
            row = lax.rem(c, n_yb) * wx + c // n_yb
            value = press[pl.ds(row, 1), :]
            value = jnp.where(sub48 == s, jnp.broadcast_to(value, (48, BLK)), 0.0)
            lefts.append(jnp.where(sub48 == s + 24, 1.0, value).astype(BF16))
            rights.append(wts[t])
        return acc + lax.dot_general(
            jnp.concatenate(lefts, axis=1), jnp.concatenate(rights, axis=1),
            (((1,), (1,)), ((), ())), preferred_element_type=F32,
        )

    acc = lax.fori_loop(0, n_tiles // group, sample, jnp.zeros((48, BLK), F32))
    answer = (acc[0:24] / jnp.maximum(acc[24:48], 1.0)).astype(BF16).astype(F32)

    back = []
    for n, (a, b) in enumerate(NEAR):
        rows = slice(8 * n, 8 * n + 2)
        if n == OWN:
            ret[rows, :] = answer[2 * n : 2 * n + 2]
        else:
            anss[rows, :] = answer[2 * n : 2 * n + 2]
    for n, (a, b) in enumerate(NEAR):
        if n != OWN:
            i = len(back)
            back.append(
                pltpu.make_async_remote_copy(
                    src_ref=anss.at[pl.ds(8 * n, 8)], dst_ref=ret.at[pl.ds(8 * n, 8)],
                    send_sem=ret_s.at[i], recv_sem=ret_r.at[i],
                    device_id=dev(a, b, -1), device_id_type=MESH,
                )
            )
            back[-1].start()
    sub32 = lax.broadcasted_iota(jnp.int32, (32, BLK), 0)
    lane32 = lax.broadcasted_iota(jnp.int32, (32, BLK), 1)
    wanted = jnp.full((32, BLK), -1, jnp.int32)
    for n in range(9):
        wanted = jnp.where(sub32 == first[n], 8 * n, wanted)
        wanted = jnp.where(sub32 == second[n], 8 * n + 1, wanted)
    mine = jnp.where(wanted == lane32, 1.0, 0.0).astype(BF16)
    for c in pay + halo:
        c.wait_send()
    for c in back:
        c.wait_recv()
    result = jnp.dot(mine, ret[...].astype(BF16), preferred_element_type=F32)
    eo_ref[...] = result[0:n_blk]
    for yb in range(n_yb):
        o_copy(yb).wait()
    for c in back:
        c.wait_send()


def per_device(
    elem_volume, elem_velocity, elem_energy, elem_mat, elem_dest, tile_slot, tile_cell,
    tile_weight, tile_count, cell_state, mat_props,
):
    gx, gy = lax.axis_size("gx"), lax.axis_size("gy")
    n_blk = elem_dest.shape[0]
    n_tiles = tile_weight.shape[0]
    wx, lanes = cell_state.shape[1], cell_state.shape[2]
    n_yb = lanes // BLK
    rows_q = 16 * wx + 16
    vmem = pl.BlockSpec(memory_space=pltpu.VMEM)
    smem = pl.BlockSpec(memory_space=pltpu.SMEM)
    hbm = pl.BlockSpec(memory_space=pl.ANY)
    dma = pltpu.SemaphoreType.DMA
    out, eo = pl.pallas_call(
        functools.partial(kernel, (gx, gy, n_blk, n_tiles, wx, n_yb)),
        out_shape=(
            jax.ShapeDtypeStruct((NQ * wx, lanes), F32),
            jax.ShapeDtypeStruct((n_blk, BLK), F32),
        ),
        in_specs=[vmem] * 5 + [smem] * 5 + [hbm] * 2,
        out_specs=(hbm, vmem),
        scratch_shapes=[
            pltpu.VMEM((n_tiles, BLK, BLK), BF16),
            pltpu.VMEM((n_yb + 2, rows_q, BLK), F32),
            pltpu.VMEM((n_yb, 16 * wx, BLK), F32),
            pltpu.VMEM((16 * n_tiles, BLK), F32),
            pltpu.VMEM((NQ // 2, 2 * n_tiles, 2 * BLK), BF16),
            pltpu.VMEM((n_yb * wx, BLK), F32),
            pltpu.VMEM((n_blk, 16, BLK), F32),
            pltpu.VMEM((n_blk, 16, BLK), BF16),
            pltpu.VMEM((n_blk, 16, BLK), BF16),
            pltpu.VMEM((2, n_yb, 16, BLK), BF16),
            pltpu.VMEM((2, n_yb, 16, BLK), BF16),
            pltpu.VMEM((2, NQ // 2 + 1, wx, BLK), BF16),
            pltpu.VMEM((2, NQ // 2 + 1, wx, BLK), BF16),
            pltpu.VMEM((128, BLK), F32),
            pltpu.VMEM((128, BLK), F32),
            dma((4,)), dma((n_yb,)), dma((n_yb,)),
            dma((8,)), dma((8,)), dma((2,)), dma((2,)), dma((2,)), dma((2,)), dma((8,)), dma((8,)),
        ],
        compiler_params=pltpu.CompilerParams(
            collective_id=0, has_side_effects=True, vmem_limit_bytes=56 * 1024 * 1024
        ),
    )(
        elem_volume.reshape(n_blk, BLK), elem_velocity, elem_energy.reshape(n_blk, BLK),
        elem_mat.reshape(n_blk, BLK), tile_cell.reshape(1, n_tiles),
        elem_dest, tile_slot, tile_cell, tile_count, mat_props,
        tile_weight, cell_state.reshape(NQ * wx, lanes),
    )
    return out.reshape(NQ, wx, lanes), eo.astype(BF16).reshape(n_blk * BLK)


def solution(mesh):
    both = ("gx", "gy")
    return jax.shard_map(
        per_device,
        mesh=mesh,
        in_specs=(
            P(both), P(None, both), P(both), P(both), P(both), P(both), P(both),
            P(both, None, None), P(both), P(None, "gx", "gy"), P(),
        ),
        out_specs=(P(None, "gx", "gy"), P(both)),
        check_vma=False,
    )
```

```python
import functools

import jax
import jax.numpy as jnp
from jax import lax
from jax.experimental import pallas as pl
from jax.experimental.pallas import tpu as pltpu
from jax.sharding import PartitionSpec as P

MAT = 8
NQ = 12
NZ = 64
BLK = 128
CAP = 2
TIME_STEP = 0.8
NEAR = [(a, b) for a in range(3) for b in range(3)]
OWN = 4
F32 = jnp.float32
BF16 = jnp.bfloat16
MESH = pl.DeviceIdType.MESH


def kernel(
    dims,
    vol, vel, ene, mat, cell_v, dest_s, slot_s, cell_s, count_s, props_s, w_hbm, state_hbm,
    f_ref, eo_ref,
    wts, q_ref, xe, fe, loc_s, row_s, s_ref, c_ref, press, blk, outg, recv, xs, xr, ys, yr, anss, ret,
    w_sem, q_sem, pay_s, pay_r, hx_s, hx_r, hy_s, hy_r, ret_s, ret_r,
):
    gx, gy, n_blk, n_tiles, wx, n_yb = dims
    px = lax.axis_index("gx")
    py = lax.axis_index("gy")
    group = 16
    pitch = n_tiles + 1
    bits_y, bits_b, bits_x = gy.bit_length() - 1, n_yb.bit_length() - 1, wx.bit_length() - 1
    assert (gx & (gx - 1), gy, n_yb, wx, CAP) == (0, 1 << bits_y, 1 << bits_b, 1 << bits_x, 2)
    n_chunk = 4
    tiles_chunk = n_tiles // n_chunk
    pad = 8
    row_x = pad + NQ * wx
    row_y = row_x + wx

    def dev(a, b, sign):
        return (lax.rem(px + sign * (a - 1) + gx, gx), lax.rem(py + sign * (b - 1) + gy, gy))

    def w_copy(i):
        part = pl.ds(i * tiles_chunk, tiles_chunk)
        return pltpu.make_async_copy(w_hbm.at[part], wts.at[part], w_sem.at[i])

    def q_copy(yb):
        return pltpu.make_async_copy(
            state_hbm.at[:, pl.ds(yb * BLK, BLK)],
            q_ref.at[yb + 1, pl.ds(pad, NQ * wx)],
            q_sem.at[yb],
        )

    ret[...] = jnp.zeros(ret.shape, F32)
    barrier = pltpu.get_barrier_semaphore()
    for a, b in NEAR:
        if (a, b) != (1, 1):
            pl.semaphore_signal(barrier, inc=1, device_id=dev(a, b, 1), device_id_type=MESH)
    for i in range(n_chunk):
        w_copy(i).start()

    sub8 = lax.broadcasted_iota(jnp.int32, (8, BLK), 0)
    dens = [props_s[0, m] for m in range(MAT)]
    stiff = [props_s[1, m] for m in range(MAT)]
    dens_col = jnp.zeros((8, BLK), F32)
    for m in range(MAT):
        dens_col = jnp.where(sub8 == m, dens[m], dens_col)
    blk[...] = jnp.zeros(blk.shape, F32)
    for j in range(n_blk):
        hit = jnp.broadcast_to(mat[j : j + 1, :], (8, BLK)) == sub8
        v = vol[j : j + 1, :]
        blk[j, 0:8, :] = jnp.where(hit, jnp.broadcast_to(v, (8, BLK)), 0.0)
        mass = v * jnp.sum(jnp.where(hit, dens_col, 0.0), axis=0, keepdims=True)
        blk[j, 8:11, :] = mass * vel[:, j * BLK : (j + 1) * BLK]
        blk[j, 11:12, :] = mass * ene[j : j + 1, :]
    first, second = [], []
    keys = []
    for j in range(n_blk):
        d = dest_s[j]
        ka = ((d >> bits_y) - px + 1) & (gx - 1)
        kb = (d - py + 1) & (gy - 1)
        keys.append(ka * 3 + kb)
    for n in range(9):
        low = jnp.int32(0)
        total = jnp.int32(0)
        for j in reversed(range(n_blk)):
            same = keys[j] == n
            low = jnp.where(same, jnp.int32(j), low)
            total = total + jnp.where(same, jnp.int32(j), jnp.int32(0))
        first.append(low)
        second.append(jnp.minimum(total - low, n_blk - 1))
    for n in range(9):
        for rank, src in ((0, first[n]), (1, second[n])):
            value = blk[src].astype(BF16)
            if n == OWN:
                recv[2 * n + rank] = value
            else:
                outg[2 * n + rank] = value

    pl.semaphore_wait(barrier, 8)
    pay = []
    for n, (a, b) in enumerate(NEAR):
        if n != OWN:
            i = len(pay)
            pay.append(
                pltpu.make_async_remote_copy(
                    src_ref=outg.at[pl.ds(2 * n, 2)], dst_ref=recv.at[pl.ds(2 * n, 2)],
                    send_sem=pay_s.at[i], recv_sem=pay_r.at[i],
                    device_id=dev(a, b, 1), device_id_type=MESH,
                )
            )
            pay[-1].start()

    def load_state(yb, carry):
        q_copy(yb).start()
        return carry

    lax.fori_loop(0, n_yb, load_state, 0)

    rows_all = q_ref.shape[1]
    n_rows = 16 * wx

    def clear_end(i, carry):
        at = pl.multiple_of(i * 8, 8)
        q_ref[0, pl.ds(at, 8), :] = jnp.zeros((8, BLK), F32)
        q_ref[n_yb + 1, pl.ds(at, 8), :] = jnp.zeros((8, BLK), F32)
        return carry

    lax.fori_loop(0, rows_all // 8, clear_end, 0)

    def clear_tail(yb, carry):
        q_ref[yb + 1, 0:pad, :] = jnp.zeros((pad, BLK), F32)
        tail = rows_all - (row_y + wx)
        q_ref[yb + 1, row_y + wx : rows_all, :] = jnp.zeros((tail, BLK), F32)
        return carry

    lax.fori_loop(0, n_yb, clear_tail, 0)
    anss[...] = jnp.zeros(anss.shape, F32)

    def clear_edge(yb, carry):
        for e in range(2):
            xe[e, yb] = jnp.zeros((16, BLK), F32)
            fe[e, yb] = jnp.zeros((16, BLK), F32)
        return carry

    lax.fori_loop(0, n_yb, clear_edge, 0)

    for c in pay:
        c.wait_recv()
    for i in range(n_chunk):
        w_copy(i).wait()

    count = count_s[0]

    def local_slot(t):
        s = slot_s[t]
        a = (px + 1 - (s >> (bits_y + 1))) & (gx - 1)
        b = (py + 1 - (s >> 1)) & (gy - 1)
        return jnp.minimum(a * 6 + b * 2 + (s & 1), n_blk - 1)

    def contrib(i, carry):
        for g in range(group):
            t = i * group + g
            at = local_slot(t)
            loc_s[t] = jnp.where(t < count, at, jnp.int32(100))
            cell = cell_s[t]
            row_s[t] = ((cell & (n_yb - 1)) << bits_x) + (cell >> bits_b)
            c = jnp.dot(recv[at], wts[t], preferred_element_type=F32)
            s_ref[pl.ds(t, 16, stride=pitch), :] = c
        return carry

    lax.fori_loop(0, n_tiles // group, contrib, 0)

    for p in range(NQ // 2):
        for h in range(2):
            value = s_ref[pl.ds((2 * p + h) * pitch, n_tiles), :]
            high = value.astype(BF16)
            c_ref[p, 0:n_tiles, h * BLK : (h + 1) * BLK] = high
            c_ref[p, n_tiles : 2 * n_tiles, h * BLK : (h + 1) * BLK] = (
                value - high.astype(F32)
            ).astype(BF16)

    lane_t = lax.broadcasted_iota(jnp.int32, (1, n_tiles), 1)
    cell_m = jnp.broadcast_to(jnp.where(lane_t < count, cell_v[...], -1), (wx, n_tiles))
    cell_at = lax.broadcasted_iota(jnp.int32, (wx, n_tiles), 0) * n_yb

    def deposit(one, two):
        picks = []
        for yb in (one, two):
            q_copy(yb).wait()
            picks.append(jnp.where(cell_m == cell_at + yb, 1.0, 0.0).astype(BF16))
        left = jnp.concatenate(
            [jnp.concatenate([pick, pick], axis=1) for pick in picks], axis=0
        )
        mass = [jnp.ones((wx, BLK), F32) for _ in range(2)]
        moving = [[], []]
        for p in range(NQ // 2):
            both = jnp.dot(left, c_ref[p], preferred_element_type=F32)
            for k, yb in enumerate((one, two)):
                for h in range(2):
                    r = 2 * p + h
                    rows = pl.ds(pad + r * wx, wx)
                    value = (
                        q_ref[yb + 1, rows, :]
                        + both[k * wx : (k + 1) * wx, h * BLK : (h + 1) * BLK]
                    )
                    q_ref[yb + 1, rows, :] = value
                    xe[0, yb, r : r + 1, :] = value[0:1]
                    xe[1, yb, r : r + 1, :] = value[wx - 1 : wx]
                    if r < MAT:
                        mass[k] = mass[k] + dens[r] * value
                    elif r < MAT + 2:
                        moving[k].append(value)
        for k, yb in enumerate((one, two)):
            scale = (0.5 * TIME_STEP) / mass[k]
            u = moving[k][0] * scale
            q_ref[yb + 1, pl.ds(row_x, wx), :] = u
            q_ref[yb + 1, pl.ds(row_y, wx), :] = moving[k][1] * scale
            xe[0, yb, NQ : NQ + 1, :] = u[0:1]
            xe[1, yb, NQ : NQ + 1, :] = u[wx - 1 : wx]
            for e in range(2):
                xs[e, yb] = xe[e, yb].astype(BF16)

    deposit(0, n_yb - 1)

    lane = lax.broadcasted_iota(jnp.int32, (wx, BLK), 1)
    upper = lane >= NZ

    def rows_of(r):
        return pl.ds(pad + r * wx, wx)

    def pair(yb, p, top):
        if p < NQ // 2:
            one, two = q_ref[yb + 1, rows_of(2 * p), :], q_ref[yb + 1, rows_of(2 * p + 1), :]
        else:
            one = q_ref[yb + 1, pl.ds(row_y, wx), :]
            two = one
        turned = pltpu.roll(one, NZ, axis=1)
        return jnp.where(upper, two, turned) if top else jnp.where(upper, turned, two)

    for p in range(NQ // 2 + 1):
        ys[0, p] = pair(0, p, False).astype(BF16)
        ys[1, p] = pair(n_yb - 1, p, True).astype(BF16)
    halo = []
    for e, b in ((0, 0), (1, 2)):
        halo.append(
            pltpu.make_async_remote_copy(
                src_ref=ys.at[e], dst_ref=yr.at[1 - e], send_sem=hy_s.at[e], recv_sem=hy_r.at[1 - e],
                device_id=dev(1, b, 1), device_id_type=MESH,
            )
        )
        halo[-1].start()

    def deposit_inner(i, carry):
        deposit(2 * i + 1, 2 * i + 2)
        return carry

    lax.fori_loop(0, n_yb // 2 - 1, deposit_inner, 0)

    for e, a in ((0, 0), (1, 2)):
        halo.append(
            pltpu.make_async_remote_copy(
                src_ref=xs.at[e], dst_ref=xr.at[1 - e], send_sem=hx_s.at[e], recv_sem=hx_r.at[1 - e],
                device_id=dev(a, 1, 1), device_id_type=MESH,
            )
        )
        halo[-1].start()

    half = wx // 2
    sub = lax.broadcasted_iota(jnp.int32, (half, BLK), 0)
    lane_h = lax.broadcasted_iota(jnp.int32, (half, BLK), 1)
    upper_h = lane_h >= NZ

    def remap(yb, carry):
        for part in range(2):
            x0 = part * half

            def at(base, shift=0):
                return pl.ds(base + x0 + shift, half)

            ux = q_ref[yb + 1, at(row_x), :]
            lo = q_ref[yb + 1, at(row_x, -1), :] + ux
            hi = ux + q_ref[yb + 1, at(row_x, 1), :]
            if part == 0:
                lo = jnp.where(sub == 0, 0.0, lo)
            else:
                hi = jnp.where(sub == half - 1, 0.0, hi)
            uy = q_ref[yb + 1, at(row_y), :]
            prev, after = q_ref[yb, at(row_y), :], q_ref[yb + 2, at(row_y), :]
            y_hi = uy + pltpu.roll(jnp.where(upper_h, uy, after), NZ, axis=1)
            y_lo = uy + pltpu.roll(jnp.where(upper_h, prev, uy), NZ, axis=1)
            place = lane_h + yb * BLK
            y_lo = jnp.where(place < NZ, 0.0, y_lo)
            y_hi = jnp.where(place >= n_yb * BLK - NZ, 0.0, y_hi)
            c_xm = jnp.maximum(lo, 0.0)
            c_xp = -jnp.minimum(hi, 0.0)
            c_ym = jnp.maximum(y_lo, 0.0)
            c_yp = -jnp.minimum(y_hi, 0.0)
            c_0 = (1.0 - jnp.maximum(hi, 0.0) + jnp.minimum(lo, 0.0)) - (
                jnp.maximum(y_hi, 0.0) - jnp.minimum(y_lo, 0.0)
            )
            t_p = pltpu.roll(c_yp, NZ, axis=1)
            t_m = pltpu.roll(c_ym, NZ, axis=1)
            own = jnp.where(upper_h, t_p, t_m)
            other = jnp.where(upper_h, t_m, t_p)
            acc = jnp.zeros((half, BLK), F32)
            for r in range(NQ):
                base = pad + r * wx
                q = q_ref[yb + 1, at(base), :]
                beside = jnp.where(upper_h, q_ref[yb, at(base), :], q_ref[yb + 2, at(base), :])
                fresh = (
                    c_0 * q
                    + c_xm * q_ref[yb + 1, at(base, -1), :]
                    + c_xp * q_ref[yb + 1, at(base, 1), :]
                    + pltpu.roll(own * q + other * beside, NZ, axis=1)
                )
                f_ref[yb, pl.ds(r * wx + x0, half), :] = fresh
                if part == 0:
                    fe[0, yb, r : r + 1, :] = fresh[0:1]
                else:
                    fe[1, yb, r : r + 1, :] = fresh[half - 1 : half]
                if r < MAT:
                    acc = acc + fresh * (stiff[r] + (0.5 * stiff[r]) * fresh)
                elif r == NQ - 1:
                    acc = acc + 0.4 * fresh
            press[pl.ds(pl.multiple_of(yb * wx + x0, half), half), :] = acc.astype(BF16).astype(F32)
        return carry

    lax.fori_loop(0, n_yb, remap, 0)

    for c in halo[:2]:
        c.wait_recv()
    has = [
        jnp.where(py > 0, 1.0, 0.0).astype(F32),
        jnp.where(py < gy - 1, 1.0, 0.0).astype(F32),
    ]
    for e, yb in ((0, 0), (1, n_yb - 1)):
        inside = jnp.logical_not(upper) if e == 0 else upper
        speed = q_ref[yb + 1, pl.ds(row_y, wx), :] + has[e] * yr[e, NQ // 2].astype(F32)
        speed = jnp.where(inside, speed, 0.0)
        pos, neg = jnp.maximum(speed, 0.0), jnp.minimum(speed, 0.0)
        w_far, w_own = (has[e] * pos, neg) if e == 0 else (-has[e] * neg, -pos)
        acc = jnp.zeros((wx, BLK), F32)
        for p in range(NQ // 2):
            packed = yr[e, p].astype(F32)
            for h in range(2):
                r = 2 * p + h
                far = packed if h == 0 else pltpu.roll(packed, NZ, axis=1)
                rows = pl.ds(r * wx, wx)
                fresh = f_ref[yb, rows, :] + (w_far * far + w_own * q_ref[yb + 1, rows_of(r), :])
                f_ref[yb, rows, :] = fresh
                fe[0, yb, r : r + 1, :] = fresh[0:1]
                fe[1, yb, r : r + 1, :] = fresh[wx - 1 : wx]
                if r < MAT:
                    acc = acc + fresh * (stiff[r] + (0.5 * stiff[r]) * fresh)
                elif r == NQ - 1:
                    acc = acc + 0.4 * fresh
        press[yb * wx : (yb + 1) * wx, :] = acc.astype(BF16).astype(F32)

    for c in halo[2:]:
        c.wait_recv()
    sub16 = lax.broadcasted_iota(jnp.int32, (16, BLK), 0)
    lin = jnp.zeros((16, BLK), F32)
    for m in range(MAT):
        lin = jnp.where(sub16 == m, stiff[m], lin)
    quad = 0.5 * lin
    lin = jnp.where(sub16 == NQ - 1, 0.4, lin)
    has = [
        jnp.where(px > 0, 1.0, 0.0).astype(F32),
        jnp.where(px < gx - 1, 1.0, 0.0).astype(F32),
    ]

    def border_x(yb, carry):
        for e, x in ((0, 0), (1, wx - 1)):
            far = xr[e, yb].astype(F32) * has[e]
            q = xe[e, yb]
            speed = q[NQ : NQ + 1] + far[NQ : NQ + 1]
            pos, neg = jnp.maximum(speed, 0.0), jnp.minimum(speed, 0.0)
            change = (pos * far + neg * q) if e == 0 else -(pos * q + neg * far)
            rows = pl.ds(x, 16, stride=wx)
            fresh = fe[e, yb] + change
            f_ref[yb, rows, :] = fresh
            terms = jnp.where(sub16 < NQ, fresh * (lin + quad * fresh), 0.0)
            value = jnp.sum(terms, axis=0, keepdims=True)
            press[pl.ds(yb * wx + x, 1), :] = value.astype(BF16).astype(F32)
        return carry

    lax.fori_loop(0, n_yb, border_x, 0)

    sub24 = lax.broadcasted_iota(jnp.int32, (24, BLK), 0)

    def sample(i, acc):
        lefts, rights = [], []
        for g in range(group):
            t = i * group + g
            hit = sub24 == loc_s[t]
            value = jnp.broadcast_to(press[pl.ds(row_s[t], 1), :], (24, BLK))
            lefts.append(
                jnp.concatenate(
                    [jnp.where(hit, value, 0.0), jnp.where(hit, 1.0, 0.0)], axis=0
                ).astype(BF16)
            )
            rights.append(wts[t])
        return acc + lax.dot_general(
            jnp.concatenate(lefts, axis=1), jnp.concatenate(rights, axis=1),
            (((1,), (1,)), ((), ())), preferred_element_type=F32,
        )

    acc = lax.fori_loop(0, n_tiles // group, sample, jnp.zeros((48, BLK), F32))
    answer = (acc[0:24] / jnp.maximum(acc[24:48], 1.0)).astype(BF16).astype(F32)

    back = []
    for n, (a, b) in enumerate(NEAR):
        rows = slice(8 * n, 8 * n + 2)
        if n == OWN:
            ret[rows, :] = answer[2 * n : 2 * n + 2]
        else:
            anss[rows, :] = answer[2 * n : 2 * n + 2]
    for n, (a, b) in enumerate(NEAR):
        if n != OWN:
            i = len(back)
            back.append(
                pltpu.make_async_remote_copy(
                    src_ref=anss.at[pl.ds(8 * n, 8)], dst_ref=ret.at[pl.ds(8 * n, 8)],
                    send_sem=ret_s.at[i], recv_sem=ret_r.at[i],
                    device_id=dev(a, b, -1), device_id_type=MESH,
                )
            )
            back[-1].start()
    sub32 = lax.broadcasted_iota(jnp.int32, (32, BLK), 0)
    lane32 = lax.broadcasted_iota(jnp.int32, (32, BLK), 1)
    wanted = jnp.full((32, BLK), -1, jnp.int32)
    for n in range(9):
        wanted = jnp.where(sub32 == first[n], 8 * n, wanted)
        wanted = jnp.where(sub32 == second[n], 8 * n + 1, wanted)
    mine = jnp.where(wanted == lane32, 1.0, 0.0).astype(BF16)
    for c in pay + halo:
        c.wait_send()
    for c in back:
        c.wait_recv()
    result = jnp.dot(mine, ret[...].astype(BF16), preferred_element_type=F32)
    eo_ref[...] = result[0:n_blk]
    for c in back:
        c.wait_send()


def write_out(n_yb, rows, f_ref, eo_ref, out_ref, ep_ref, sem):
    copies = [
        pltpu.make_async_copy(
            f_ref.at[yb, pl.ds(0, rows)], out_ref.at[:, pl.ds(yb * BLK, BLK)], sem.at[yb]
        )
        for yb in range(n_yb)
    ]
    for c in copies:
        c.start()
    ep_ref[...] = eo_ref[...].astype(BF16)
    for c in copies:
        c.wait()


def per_device(
    elem_volume, elem_velocity, elem_energy, elem_mat, elem_dest, tile_slot, tile_cell,
    tile_weight, tile_count, cell_state, mat_props,
):
    gx, gy = lax.axis_size("gx"), lax.axis_size("gy")
    n_blk = elem_dest.shape[0]
    n_tiles = tile_weight.shape[0]
    wx, lanes = cell_state.shape[1], cell_state.shape[2]
    n_yb = lanes // BLK
    rows_q = 16 * wx + 16
    vmem = pl.BlockSpec(memory_space=pltpu.VMEM)
    smem = pl.BlockSpec(memory_space=pltpu.SMEM)
    hbm = pl.BlockSpec(memory_space=pltpu.HBM)
    dma = pltpu.SemaphoreType.DMA
    fresh, eo = pl.pallas_call(
        functools.partial(kernel, (gx, gy, n_blk, n_tiles, wx, n_yb)),
        out_shape=(
            pltpu.VMEM((n_yb, 16 * wx, BLK), F32),
            pltpu.VMEM((n_blk, BLK), F32),
        ),
        in_specs=[vmem] * 5 + [smem] * 5 + [hbm] * 2,
        out_specs=(vmem, vmem),
        scratch_shapes=[
            pltpu.VMEM((n_tiles, BLK, BLK), BF16),
            pltpu.VMEM((n_yb + 2, rows_q, BLK), F32),
            pltpu.VMEM((2, n_yb, 16, BLK), F32),
            pltpu.VMEM((2, n_yb, 16, BLK), F32),
            pltpu.SMEM((n_tiles,), jnp.int32),
            pltpu.SMEM((n_tiles,), jnp.int32),
            pltpu.VMEM((16 * n_tiles + 24, BLK), F32),
            pltpu.VMEM((NQ // 2, 2 * n_tiles, 2 * BLK), BF16),
            pltpu.VMEM((n_yb * wx, BLK), F32),
            pltpu.VMEM((n_blk, 16, BLK), F32),
            pltpu.VMEM((n_blk, 16, BLK), BF16),
            pltpu.VMEM((n_blk, 16, BLK), BF16),
            pltpu.VMEM((2, n_yb, 16, BLK), BF16),
            pltpu.VMEM((2, n_yb, 16, BLK), BF16),
            pltpu.VMEM((2, NQ // 2 + 1, wx, BLK), BF16),
            pltpu.VMEM((2, NQ // 2 + 1, wx, BLK), BF16),
            pltpu.VMEM((128, BLK), F32),
            pltpu.VMEM((128, BLK), F32),
            dma((4,)), dma((n_yb,)),
            dma((8,)), dma((8,)), dma((2,)), dma((2,)), dma((2,)), dma((2,)), dma((8,)), dma((8,)),
        ],
        compiler_params=pltpu.CompilerParams(
            collective_id=0, has_side_effects=True, vmem_limit_bytes=67043328 - 8388608 - 16384
        ),
    )(
        elem_volume.reshape(n_blk, BLK), elem_velocity, elem_energy.reshape(n_blk, BLK),
        elem_mat.reshape(n_blk, BLK), tile_cell.reshape(1, n_tiles),
        elem_dest, tile_slot, tile_cell, tile_count, mat_props,
        tile_weight, cell_state.reshape(NQ * wx, lanes),
    )
    out, pressure = pl.pallas_call(
        functools.partial(write_out, n_yb, NQ * wx),
        out_shape=(
            jax.ShapeDtypeStruct((NQ * wx, lanes), F32),
            jax.ShapeDtypeStruct((n_blk, BLK), BF16),
        ),
        in_specs=[vmem, vmem],
        out_specs=(hbm, vmem),
        scratch_shapes=[dma((n_yb,))],
        compiler_params=pltpu.CompilerParams(vmem_limit_bytes=4 * 1024 * 1024),
    )(fresh, eo)
    return out.reshape(NQ, wx, lanes), pressure.reshape(n_blk * BLK)


def solution(mesh):
    both = ("gx", "gy")
    return jax.shard_map(
        per_device,
        mesh=mesh,
        in_specs=(
            P(both), P(None, both), P(both), P(both), P(both), P(both), P(both),
            P(both, None, None), P(both), P(None, "gx", "gy"), P(),
        ),
        out_specs=(P(None, "gx", "gy"), P(both)),
        check_vma=False,
    )
```

```python
import functools

import jax
import jax.numpy as jnp
from jax import lax
from jax.experimental import pallas as pl
from jax.experimental.pallas import tpu as pltpu
from jax.sharding import PartitionSpec as P

MAT = 8
NQ = 12
NZ = 64
BLK = 128
CAP = 2
TIME_STEP = 0.8
NEAR = [(a, b) for a in range(3) for b in range(3)]
OWN = 4
F32 = jnp.float32
BF16 = jnp.bfloat16
MESH = pl.DeviceIdType.MESH


def kernel(
    dims,
    vol_h, vel_h, ene_h, mat_h, cell_h, dest_h, slot_h, cell1_h, count_h, props_h, w_hbm, state_hbm,
    f_ref, eo_ref,
    vol, vel, ene, mat, cell_v, dest_s, slot_s, cell_s, count_s, props_s,
    wts, q_ref, xe, fe, at_s, loc_s, row_s, s_ref, c_ref, press, blk, outg, recv, xs, xr, ys, yr, anss, ret,
    in_sem, w_sem, q_sem, pay_s, pay_r, hx_s, hx_r, hy_s, hy_r, ret_s, ret_r,
):
    gx, gy, n_blk, n_tiles, wx, n_yb = dims
    px = lax.axis_index("gx")
    py = lax.axis_index("gy")
    group = 16
    pitch = n_tiles + 1
    bits_y, bits_b, bits_x = gy.bit_length() - 1, n_yb.bit_length() - 1, wx.bit_length() - 1
    assert (gx & (gx - 1), gy, n_yb, wx, CAP) == (0, 1 << bits_y, 1 << bits_b, 1 << bits_x, 2)
    n_chunk = 4
    tiles_chunk = n_tiles // n_chunk
    pad = 8
    row_x = pad + NQ * wx
    row_y = row_x + wx

    def dev(a, b, sign):
        return (lax.rem(px + sign * (a - 1) + gx, gx), lax.rem(py + sign * (b - 1) + gy, gy))

    def w_copy(i):
        part = pl.ds(i * tiles_chunk, tiles_chunk)
        return pltpu.make_async_copy(w_hbm.at[part], wts.at[part], w_sem.at[i])

    def q_copy(yb):
        return pltpu.make_async_copy(
            state_hbm.at[:, pl.ds(yb * BLK, BLK)],
            q_ref.at[yb + 1, pl.ds(pad, NQ * wx)],
            q_sem.at[yb],
        )

    ret[...] = jnp.zeros(ret.shape, F32)
    barrier = pltpu.get_barrier_semaphore()
    for a, b in NEAR:
        if (a, b) != (1, 1):
            pl.semaphore_signal(barrier, inc=1, device_id=dev(a, b, 1), device_id_type=MESH)
    small = [
        pltpu.make_async_copy(src, dst, in_sem.at[i])
        for i, (src, dst) in enumerate((
            (dest_h, dest_s), (props_h, props_s), (vol_h, vol), (mat_h, mat), (vel_h, vel),
            (ene_h, ene), (slot_h, slot_s), (cell1_h, cell_s), (count_h, count_s), (cell_h, cell_v),
        ))
    ]
    for c in small:
        c.start()
    for i in range(n_chunk):
        w_copy(i).start()
    for c in small:
        c.wait()

    sub8 = lax.broadcasted_iota(jnp.int32, (8, BLK), 0)
    dens = [props_s[0, m] for m in range(MAT)]
    stiff = [props_s[1, m] for m in range(MAT)]
    dens_col = jnp.zeros((8, BLK), F32)
    for m in range(MAT):
        dens_col = jnp.where(sub8 == m, dens[m], dens_col)
    blk[...] = jnp.zeros(blk.shape, F32)
    for j in range(n_blk):
        hit = jnp.broadcast_to(mat[j : j + 1, :], (8, BLK)) == sub8
        v = vol[j : j + 1, :]
        blk[j, 0:8, :] = jnp.where(hit, jnp.broadcast_to(v, (8, BLK)), 0.0)
        mass = v * jnp.sum(jnp.where(hit, dens_col, 0.0), axis=0, keepdims=True)
        blk[j, 8:11, :] = mass * vel[:, j * BLK : (j + 1) * BLK]
        blk[j, 11:12, :] = mass * ene[j : j + 1, :]
    first, second = [], []
    keys = []
    for j in range(n_blk):
        d = dest_s[j]
        ka = ((d >> bits_y) - px + 1) & (gx - 1)
        kb = (d - py + 1) & (gy - 1)
        keys.append(ka * 3 + kb)
    for n in range(9):
        low = jnp.int32(0)
        total = jnp.int32(0)
        for j in reversed(range(n_blk)):
            same = keys[j] == n
            low = jnp.where(same, jnp.int32(j), low)
            total = total + jnp.where(same, jnp.int32(j), jnp.int32(0))
        first.append(low)
        second.append(jnp.minimum(total - low, n_blk - 1))
    for n in range(9):
        for rank, src in ((0, first[n]), (1, second[n])):
            value = blk[src].astype(BF16)
            if n == OWN:
                recv[2 * n + rank] = value
            else:
                outg[2 * n + rank] = value

    pl.semaphore_wait(barrier, 8)
    pay = []
    for n, (a, b) in enumerate(NEAR):
        if n != OWN:
            i = len(pay)
            pay.append(
                pltpu.make_async_remote_copy(
                    src_ref=outg.at[pl.ds(2 * n, 2)], dst_ref=recv.at[pl.ds(2 * n, 2)],
                    send_sem=pay_s.at[i], recv_sem=pay_r.at[i],
                    device_id=dev(a, b, 1), device_id_type=MESH,
                )
            )
            pay[-1].start()

    def load_state(yb, carry):
        q_copy(yb).start()
        return carry

    lax.fori_loop(0, n_yb, load_state, 0)

    rows_all = q_ref.shape[1]
    n_rows = 16 * wx

    def clear_end(i, carry):
        at = pl.multiple_of(i * 8, 8)
        q_ref[0, pl.ds(at, 8), :] = jnp.zeros((8, BLK), F32)
        q_ref[n_yb + 1, pl.ds(at, 8), :] = jnp.zeros((8, BLK), F32)
        return carry

    lax.fori_loop(0, rows_all // 8, clear_end, 0)

    def clear_tail(yb, carry):
        q_ref[yb + 1, 0:pad, :] = jnp.zeros((pad, BLK), F32)
        tail = rows_all - (row_y + wx)
        q_ref[yb + 1, row_y + wx : rows_all, :] = jnp.zeros((tail, BLK), F32)
        return carry

    lax.fori_loop(0, n_yb, clear_tail, 0)
    anss[...] = jnp.zeros(anss.shape, F32)

    def clear_edge(yb, carry):
        for e in range(2):
            xe[e, yb] = jnp.zeros((16, BLK), F32)
            fe[e, yb] = jnp.zeros((16, BLK), F32)
        return carry

    lax.fori_loop(0, n_yb, clear_edge, 0)

    count = count_s[0]

    def places(i, carry):
        for g in range(8):
            t = i * 8 + g
            s = slot_s[t]
            a = (px + 1 - (s >> (bits_y + 1))) & (gx - 1)
            b = (py + 1 - (s >> 1)) & (gy - 1)
            at = jnp.minimum(a * 6 + b * 2 + (s & 1), n_blk - 1)
            at_s[t] = at
            loc_s[t] = jnp.where(t < count, at, jnp.int32(100))
            cell = cell_s[t]
            row_s[t] = ((cell & (n_yb - 1)) << bits_x) + (cell >> bits_b)
        return carry

    lax.fori_loop(0, n_tiles // 8, places, 0)

    for c in pay:
        c.wait_recv()
    for i in range(n_chunk):
        w_copy(i).wait()

    def contrib(i, carry):
        for g in range(group):
            t = i * group + g
            c = jnp.dot(recv[at_s[t]], wts[t], preferred_element_type=F32)
            s_ref[pl.ds(t, 16, stride=pitch), :] = c
        return carry

    lax.fori_loop(0, n_tiles // group, contrib, 0)

    for p in range(NQ // 2):
        for h in range(2):
            value = s_ref[pl.ds((2 * p + h) * pitch, n_tiles), :]
            high = value.astype(BF16)
            c_ref[p, 0:n_tiles, h * BLK : (h + 1) * BLK] = high
            c_ref[p, n_tiles : 2 * n_tiles, h * BLK : (h + 1) * BLK] = (
                value - high.astype(F32)
            ).astype(BF16)

    lane_t = lax.broadcasted_iota(jnp.int32, (1, n_tiles), 1)
    cell_m = jnp.broadcast_to(jnp.where(lane_t < count, cell_v[...], -1), (wx, n_tiles))
    cell_at = lax.broadcasted_iota(jnp.int32, (wx, n_tiles), 0) * n_yb

    def deposit(one, two):
        picks = []
        for yb in (one, two):
            q_copy(yb).wait()
            picks.append(jnp.where(cell_m == cell_at + yb, 1.0, 0.0).astype(BF16))
        left = jnp.concatenate(
            [jnp.concatenate([pick, pick], axis=1) for pick in picks], axis=0
        )
        mass = [jnp.ones((wx, BLK), F32) for _ in range(2)]
        moving = [[], []]
        for p in range(NQ // 2):
            both = jnp.dot(left, c_ref[p], preferred_element_type=F32)
            for k, yb in enumerate((one, two)):
                for h in range(2):
                    r = 2 * p + h
                    rows = pl.ds(pad + r * wx, wx)
                    value = (
                        q_ref[yb + 1, rows, :]
                        + both[k * wx : (k + 1) * wx, h * BLK : (h + 1) * BLK]
                    )
                    q_ref[yb + 1, rows, :] = value
                    xe[0, yb, r : r + 1, :] = value[0:1]
                    xe[1, yb, r : r + 1, :] = value[wx - 1 : wx]
                    if r < MAT:
                        mass[k] = mass[k] + dens[r] * value
                    elif r < MAT + 2:
                        moving[k].append(value)
        for k, yb in enumerate((one, two)):
            scale = (0.5 * TIME_STEP) / mass[k]
            u = moving[k][0] * scale
            q_ref[yb + 1, pl.ds(row_x, wx), :] = u
            q_ref[yb + 1, pl.ds(row_y, wx), :] = moving[k][1] * scale
            xe[0, yb, NQ : NQ + 1, :] = u[0:1]
            xe[1, yb, NQ : NQ + 1, :] = u[wx - 1 : wx]
            for e in range(2):
                xs[e, yb] = xe[e, yb].astype(BF16)

    deposit(0, n_yb - 1)

    lane = lax.broadcasted_iota(jnp.int32, (wx, BLK), 1)
    upper = lane >= NZ

    def rows_of(r):
        return pl.ds(pad + r * wx, wx)

    def pair(yb, p, top):
        if p < NQ // 2:
            one, two = q_ref[yb + 1, rows_of(2 * p), :], q_ref[yb + 1, rows_of(2 * p + 1), :]
        else:
            one = q_ref[yb + 1, pl.ds(row_y, wx), :]
            two = one
        turned = pltpu.roll(one, NZ, axis=1)
        return jnp.where(upper, two, turned) if top else jnp.where(upper, turned, two)

    for p in range(NQ // 2 + 1):
        ys[0, p] = pair(0, p, False).astype(BF16)
        ys[1, p] = pair(n_yb - 1, p, True).astype(BF16)
    halo = []
    for e, b in ((0, 0), (1, 2)):
        halo.append(
            pltpu.make_async_remote_copy(
                src_ref=ys.at[e], dst_ref=yr.at[1 - e], send_sem=hy_s.at[e], recv_sem=hy_r.at[1 - e],
                device_id=dev(1, b, 1), device_id_type=MESH,
            )
        )
        halo[-1].start()

    def deposit_inner(i, carry):
        deposit(2 * i + 1, 2 * i + 2)
        return carry

    lax.fori_loop(0, n_yb // 2 - 1, deposit_inner, 0)

    for e, a in ((0, 0), (1, 2)):
        halo.append(
            pltpu.make_async_remote_copy(
                src_ref=xs.at[e], dst_ref=xr.at[1 - e], send_sem=hx_s.at[e], recv_sem=hx_r.at[1 - e],
                device_id=dev(a, 1, 1), device_id_type=MESH,
            )
        )
        halo[-1].start()

    parts = 2
    half = wx // parts
    sub = lax.broadcasted_iota(jnp.int32, (half, BLK), 0)
    lane_h = lax.broadcasted_iota(jnp.int32, (half, BLK), 1)
    upper_h = lane_h >= NZ

    def remap(yb, carry):
        lanes = pl.ds(pl.multiple_of(yb * BLK, BLK), BLK)
        for part in range(parts):
            x0 = part * half

            def at(base, shift=0):
                return pl.ds(base + x0 + shift, half)

            ux = q_ref[yb + 1, at(row_x), :]
            lo = q_ref[yb + 1, at(row_x, -1), :] + ux
            hi = ux + q_ref[yb + 1, at(row_x, 1), :]
            if part == 0:
                lo = jnp.where(sub == 0, 0.0, lo)
            elif part == parts - 1:
                hi = jnp.where(sub == half - 1, 0.0, hi)
            uy = q_ref[yb + 1, at(row_y), :]
            prev, after = q_ref[yb, at(row_y), :], q_ref[yb + 2, at(row_y), :]
            y_hi = uy + pltpu.roll(jnp.where(upper_h, uy, after), NZ, axis=1)
            y_lo = uy + pltpu.roll(jnp.where(upper_h, prev, uy), NZ, axis=1)
            place = lane_h + yb * BLK
            y_lo = jnp.where(place < NZ, 0.0, y_lo)
            y_hi = jnp.where(place >= n_yb * BLK - NZ, 0.0, y_hi)
            c_xm = jnp.maximum(lo, 0.0)
            c_xp = -jnp.minimum(hi, 0.0)
            c_ym = jnp.maximum(y_lo, 0.0)
            c_yp = -jnp.minimum(y_hi, 0.0)
            c_0 = (1.0 - jnp.maximum(hi, 0.0) + jnp.minimum(lo, 0.0)) - (
                jnp.maximum(y_hi, 0.0) - jnp.minimum(y_lo, 0.0)
            )
            t_p = pltpu.roll(c_yp, NZ, axis=1)
            t_m = pltpu.roll(c_ym, NZ, axis=1)
            own = jnp.where(upper_h, t_p, t_m)
            other = jnp.where(upper_h, t_m, t_p)
            acc = jnp.zeros((half, BLK), F32)
            for r in range(NQ):
                base = pad + r * wx
                q = q_ref[yb + 1, at(base), :]
                beside = jnp.where(upper_h, q_ref[yb, at(base), :], q_ref[yb + 2, at(base), :])
                fresh = (
                    c_0 * q
                    + c_xm * q_ref[yb + 1, at(base, -1), :]
                    + c_xp * q_ref[yb + 1, at(base, 1), :]
                    + pltpu.roll(own * q + other * beside, NZ, axis=1)
                )
                f_ref[pl.ds(r * wx + x0, half), lanes] = fresh
                if part == 0:
                    fe[0, yb, r : r + 1, :] = fresh[0:1]
                elif part == parts - 1:
                    fe[1, yb, r : r + 1, :] = fresh[half - 1 : half]
                if r < MAT:
                    acc = acc + fresh * (stiff[r] + (0.5 * stiff[r]) * fresh)
                elif r == NQ - 1:
                    acc = acc + 0.4 * fresh
            press[pl.ds(pl.multiple_of(yb * wx + x0, half), half), :] = acc.astype(BF16).astype(F32)
        return carry

    lax.fori_loop(0, n_yb, remap, 0)

    for c in halo[:2]:
        c.wait_recv()
    has = [
        jnp.where(py > 0, 1.0, 0.0).astype(F32),
        jnp.where(py < gy - 1, 1.0, 0.0).astype(F32),
    ]
    for e, yb in ((0, 0), (1, n_yb - 1)):
        inside = jnp.logical_not(upper) if e == 0 else upper
        speed = q_ref[yb + 1, pl.ds(row_y, wx), :] + has[e] * yr[e, NQ // 2].astype(F32)
        speed = jnp.where(inside, speed, 0.0)
        pos, neg = jnp.maximum(speed, 0.0), jnp.minimum(speed, 0.0)
        w_far, w_own = (has[e] * pos, neg) if e == 0 else (-has[e] * neg, -pos)
        acc = jnp.zeros((wx, BLK), F32)
        for p in range(NQ // 2):
            packed = yr[e, p].astype(F32)
            for h in range(2):
                r = 2 * p + h
                far = packed if h == 0 else pltpu.roll(packed, NZ, axis=1)
                here = (slice(r * wx, (r + 1) * wx), slice(yb * BLK, (yb + 1) * BLK))
                fresh = f_ref[here] + (w_far * far + w_own * q_ref[yb + 1, rows_of(r), :])
                f_ref[here] = fresh
                fe[0, yb, r : r + 1, :] = fresh[0:1]
                fe[1, yb, r : r + 1, :] = fresh[wx - 1 : wx]
                if r < MAT:
                    acc = acc + fresh * (stiff[r] + (0.5 * stiff[r]) * fresh)
                elif r == NQ - 1:
                    acc = acc + 0.4 * fresh
        press[yb * wx : (yb + 1) * wx, :] = acc.astype(BF16).astype(F32)

    for c in halo[2:]:
        c.wait_recv()
    sub16 = lax.broadcasted_iota(jnp.int32, (16, BLK), 0)
    lin = jnp.zeros((16, BLK), F32)
    for m in range(MAT):
        lin = jnp.where(sub16 == m, stiff[m], lin)
    quad = 0.5 * lin
    lin = jnp.where(sub16 == NQ - 1, 0.4, lin)
    has = [
        jnp.where(px > 0, 1.0, 0.0).astype(F32),
        jnp.where(px < gx - 1, 1.0, 0.0).astype(F32),
    ]

    def border_x(i, carry):
        for yb in (2 * i, 2 * i + 1):
            lanes = pl.ds(pl.multiple_of(yb * BLK, BLK), BLK)
            for e, x in ((0, 0), (1, wx - 1)):
                far = xr[e, yb].astype(F32) * has[e]
                q = xe[e, yb]
                speed = q[NQ : NQ + 1] + far[NQ : NQ + 1]
                pos, neg = jnp.maximum(speed, 0.0), jnp.minimum(speed, 0.0)
                change = (pos * far + neg * q) if e == 0 else -(pos * q + neg * far)
                fresh = fe[e, yb] + change
                for r in range(NQ):
                    f_ref[r * wx + x : r * wx + x + 1, lanes] = fresh[r : r + 1]
                terms = jnp.where(sub16 < NQ, fresh * (lin + quad * fresh), 0.0)
                value = jnp.sum(terms, axis=0, keepdims=True)
                press[pl.ds(yb * wx + x, 1), :] = value.astype(BF16).astype(F32)
        return carry

    lax.fori_loop(0, n_yb // 2, border_x, 0)

    sub24 = lax.broadcasted_iota(jnp.int32, (24, BLK), 0)

    def sample(i, acc):
        lefts, rights = [], []
        for g in range(group):
            t = i * group + g
            hit = sub24 == loc_s[t]
            value = jnp.broadcast_to(press[pl.ds(row_s[t], 1), :], (24, BLK))
            lefts.append(
                jnp.concatenate(
                    [jnp.where(hit, value, 0.0), jnp.where(hit, 1.0, 0.0)], axis=0
                ).astype(BF16)
            )
            rights.append(wts[t])
        return acc + lax.dot_general(
            jnp.concatenate(lefts, axis=1), jnp.concatenate(rights, axis=1),
            (((1,), (1,)), ((), ())), preferred_element_type=F32,
        )

    acc = lax.fori_loop(0, n_tiles // group, sample, jnp.zeros((48, BLK), F32))
    answer = (acc[0:24] / jnp.maximum(acc[24:48], 1.0)).astype(BF16).astype(F32)

    back = []
    for n, (a, b) in enumerate(NEAR):
        rows = slice(8 * n, 8 * n + 2)
        if n == OWN:
            ret[rows, :] = answer[2 * n : 2 * n + 2]
        else:
            anss[rows, :] = answer[2 * n : 2 * n + 2]
    for n, (a, b) in enumerate(NEAR):
        if n != OWN:
            i = len(back)
            back.append(
                pltpu.make_async_remote_copy(
                    src_ref=anss.at[pl.ds(8 * n, 8)], dst_ref=ret.at[pl.ds(8 * n, 8)],
                    send_sem=ret_s.at[i], recv_sem=ret_r.at[i],
                    device_id=dev(a, b, -1), device_id_type=MESH,
                )
            )
            back[-1].start()
    sub32 = lax.broadcasted_iota(jnp.int32, (32, BLK), 0)
    lane32 = lax.broadcasted_iota(jnp.int32, (32, BLK), 1)
    wanted = jnp.full((32, BLK), -1, jnp.int32)
    for n in range(9):
        wanted = jnp.where(sub32 == first[n], 8 * n, wanted)
        wanted = jnp.where(sub32 == second[n], 8 * n + 1, wanted)
    mine = jnp.where(wanted == lane32, 1.0, 0.0).astype(BF16)
    for c in pay + halo:
        c.wait_send()
    for c in back:
        c.wait_recv()
    result = jnp.dot(mine, ret[...].astype(BF16), preferred_element_type=F32)
    eo_ref[...] = result[0:n_blk]
    for c in back:
        c.wait_send()


def write_out(f_ref, eo_ref, out_ref, ep_ref, sem):
    step = f_ref.shape[0] // sem.shape[0]
    copies = [
        pltpu.make_async_copy(f_ref.at[pl.ds(i * step, step)], out_ref.at[pl.ds(i * step, step)], sem.at[i])
        for i in range(sem.shape[0])
    ]
    for c in copies:
        c.start()
    ep_ref[...] = eo_ref[...].astype(BF16)
    for c in copies:
        c.wait()


def per_device(
    elem_volume, elem_velocity, elem_energy, elem_mat, elem_dest, tile_slot, tile_cell,
    tile_weight, tile_count, cell_state, mat_props,
):
    gx, gy = lax.axis_size("gx"), lax.axis_size("gy")
    n_blk = elem_dest.shape[0]
    n_tiles = tile_weight.shape[0]
    wx, lanes = cell_state.shape[1], cell_state.shape[2]
    n_yb = lanes // BLK
    rows_q = 16 * wx + 16
    vmem = pl.BlockSpec(memory_space=pltpu.VMEM)
    smem, i32 = pltpu.SMEM, jnp.int32
    hbm = pl.BlockSpec(memory_space=pltpu.HBM)
    dma = pltpu.SemaphoreType.DMA
    fresh, eo = pl.pallas_call(
        functools.partial(kernel, (gx, gy, n_blk, n_tiles, wx, n_yb)),
        out_shape=(
            pltpu.VMEM((NQ * wx, lanes), F32),
            pltpu.VMEM((n_blk, BLK), F32),
        ),
        in_specs=[hbm] * 12,
        out_specs=(vmem, vmem),
        scratch_shapes=[
            pltpu.VMEM((n_blk, BLK), F32), pltpu.VMEM((3, n_blk * BLK), F32),
            pltpu.VMEM((n_blk, BLK), F32), pltpu.VMEM((n_blk, BLK), i32), pltpu.VMEM((1, n_tiles), i32),
            smem((n_blk,), i32), smem((n_tiles,), i32), smem((n_tiles,), i32), smem((1,), i32), smem((2, MAT), F32),
            pltpu.VMEM((n_tiles, BLK, BLK), BF16),
            pltpu.VMEM((n_yb + 2, rows_q, BLK), F32),
            pltpu.VMEM((2, n_yb, 16, BLK), F32),
            pltpu.VMEM((2, n_yb, 16, BLK), F32),
            smem((n_tiles,), i32), smem((n_tiles,), i32), smem((n_tiles,), i32),
            pltpu.VMEM((16 * n_tiles + 24, BLK), F32),
            pltpu.VMEM((NQ // 2, 2 * n_tiles, 2 * BLK), BF16),
            pltpu.VMEM((n_yb * wx, BLK), F32),
            pltpu.VMEM((n_blk, 16, BLK), F32),
            pltpu.VMEM((n_blk, 16, BLK), BF16),
            pltpu.VMEM((n_blk, 16, BLK), BF16),
            pltpu.VMEM((2, n_yb, 16, BLK), BF16),
            pltpu.VMEM((2, n_yb, 16, BLK), BF16),
            pltpu.VMEM((2, NQ // 2 + 1, wx, BLK), BF16),
            pltpu.VMEM((2, NQ // 2 + 1, wx, BLK), BF16),
            pltpu.VMEM((128, BLK), F32),
            pltpu.VMEM((128, BLK), F32),
            dma((10,)), dma((4,)), dma((n_yb,)),
            dma((8,)), dma((8,)), dma((2,)), dma((2,)), dma((2,)), dma((2,)), dma((8,)), dma((8,)),
        ],
        compiler_params=pltpu.CompilerParams(
            collective_id=0, has_side_effects=True, vmem_limit_bytes=67043328 - 6291456 - 16384
        ),
    )(
        elem_volume.reshape(n_blk, BLK), elem_velocity, elem_energy.reshape(n_blk, BLK),
        elem_mat.reshape(n_blk, BLK), tile_cell.reshape(1, n_tiles),
        elem_dest, tile_slot, tile_cell, tile_count, mat_props,
        tile_weight, cell_state.reshape(NQ * wx, lanes),
    )
    out, pressure = pl.pallas_call(
        write_out,
        out_shape=(
            jax.ShapeDtypeStruct((NQ * wx, lanes), F32),
            jax.ShapeDtypeStruct((n_blk, BLK), BF16),
        ),
        in_specs=[vmem, vmem],
        out_specs=(hbm, vmem),
        scratch_shapes=[dma((8,))],
        compiler_params=pltpu.CompilerParams(vmem_limit_bytes=4 * 1024 * 1024),
    )(fresh, eo)
    return out.reshape(NQ, wx, lanes), pressure.reshape(n_blk * BLK)


def solution(mesh):
    both = ("gx", "gy")
    return jax.shard_map(
        per_device,
        mesh=mesh,
        in_specs=(
            P(both), P(None, both), P(both), P(both), P(both), P(both), P(both),
            P(both, None, None), P(both), P(None, "gx", "gy"), P(),
        ),
        out_specs=(P(None, "gx", "gy"), P(both)),
        check_vma=False,
    )
```

```python
import functools

import jax
import jax.numpy as jnp
from jax import lax
from jax.experimental import pallas as pl
from jax.experimental.pallas import tpu as pltpu
from jax.sharding import PartitionSpec as P

MAT = 8
NQ = 12
NZ = 64
BLK = 128
CAP = 2
TIME_STEP = 0.8
NEAR = [(a, b) for a in range(3) for b in range(3)]
OWN = 4
F32 = jnp.float32
BF16 = jnp.bfloat16
MESH = pl.DeviceIdType.MESH


def kernel(
    dims,
    vol_h, vel_h, ene_h, mat_h, cell_h, dest_h, slot_h, cell1_h, count_h, props_h, w_hbm, state_hbm,
    f_ref, eo_ref,
    vol, vel, ene, mat, cell_v, dest_s, slot_s, cell_s, count_s, props_s,
    wts, q_ref, xe, fe, at_s, loc_s, row_s, s_ref, c_ref, press, blk, outg, recv, xs, xr, ys, yr, anss, ret,
    in_sem, w_sem, q_sem, pay_s, pay_r, hx_s, hx_r, hy_s, hy_r, ret_s, ret_r,
):
    gx, gy, n_blk, n_tiles, wx, n_yb = dims
    px = lax.axis_index("gx")
    py = lax.axis_index("gy")
    group = 16
    pitch = n_tiles + 1
    bits_y, bits_b, bits_x = gy.bit_length() - 1, n_yb.bit_length() - 1, wx.bit_length() - 1
    assert (gx & (gx - 1), gy, n_yb, wx, CAP) == (0, 1 << bits_y, 1 << bits_b, 1 << bits_x, 2)
    n_chunk = 4
    tiles_chunk = n_tiles // n_chunk
    pad = 8
    row_x = pad + NQ * wx
    row_y = row_x + wx

    def dev(a, b, sign):
        return (lax.rem(px + sign * (a - 1) + gx, gx), lax.rem(py + sign * (b - 1) + gy, gy))

    def w_copy(i):
        part = pl.ds(i * tiles_chunk, tiles_chunk)
        return pltpu.make_async_copy(w_hbm.at[part], wts.at[part], w_sem.at[i])

    def q_copy(yb):
        return pltpu.make_async_copy(
            state_hbm.at[:, pl.ds(yb * BLK, BLK)],
            q_ref.at[yb + 1, pl.ds(pad, NQ * wx)],
            q_sem.at[yb],
        )

    ret[...] = jnp.zeros(ret.shape, F32)
    barrier = pltpu.get_barrier_semaphore()
    for a, b in NEAR:
        if (a, b) != (1, 1):
            pl.semaphore_signal(barrier, inc=1, device_id=dev(a, b, 1), device_id_type=MESH)
    small = [
        pltpu.make_async_copy(src, dst, in_sem.at[i])
        for i, (src, dst) in enumerate((
            (dest_h, dest_s), (props_h, props_s), (vol_h, vol), (mat_h, mat), (vel_h, vel),
            (ene_h, ene), (slot_h, slot_s), (cell1_h, cell_s), (count_h, count_s), (cell_h, cell_v),
        ))
    ]
    for c in small:
        c.start()
    for i in range(n_chunk):
        w_copy(i).start()
    for c in small:
        c.wait()

    sub8 = lax.broadcasted_iota(jnp.int32, (8, BLK), 0)
    dens = [props_s[0, m] for m in range(MAT)]
    stiff = [props_s[1, m] for m in range(MAT)]
    dens_col = jnp.zeros((8, BLK), F32)
    for m in range(MAT):
        dens_col = jnp.where(sub8 == m, dens[m], dens_col)
    blk[...] = jnp.zeros(blk.shape, F32)
    for j in range(n_blk):
        hit = jnp.broadcast_to(mat[j : j + 1, :], (8, BLK)) == sub8
        v = vol[j : j + 1, :]
        blk[j, 0:8, :] = jnp.where(hit, jnp.broadcast_to(v, (8, BLK)), 0.0)
        mass = v * jnp.sum(jnp.where(hit, dens_col, 0.0), axis=0, keepdims=True)
        blk[j, 8:11, :] = mass * vel[:, j * BLK : (j + 1) * BLK]
        blk[j, 11:12, :] = mass * ene[j : j + 1, :]
    first, second = [], []
    keys = []
    for j in range(n_blk):
        d = dest_s[j]
        ka = ((d >> bits_y) - px + 1) & (gx - 1)
        kb = (d - py + 1) & (gy - 1)
        keys.append(ka * 3 + kb)
    for n in range(9):
        low = jnp.int32(0)
        total = jnp.int32(0)
        for j in reversed(range(n_blk)):
            same = keys[j] == n
            low = jnp.where(same, jnp.int32(j), low)
            total = total + jnp.where(same, jnp.int32(j), jnp.int32(0))
        first.append(low)
        second.append(jnp.minimum(total - low, n_blk - 1))
    for n in range(9):
        for rank, src in ((0, first[n]), (1, second[n])):
            value = blk[src].astype(BF16)
            if n == OWN:
                recv[2 * n + rank] = value
            else:
                outg[2 * n + rank] = value

    pl.semaphore_wait(barrier, 8)
    pay = []
    for n, (a, b) in enumerate(NEAR):
        if n != OWN:
            i = len(pay)
            pay.append(
                pltpu.make_async_remote_copy(
                    src_ref=outg.at[pl.ds(2 * n, 2)], dst_ref=recv.at[pl.ds(2 * n, 2)],
                    send_sem=pay_s.at[i], recv_sem=pay_r.at[i],
                    device_id=dev(a, b, 1), device_id_type=MESH,
                )
            )
            pay[-1].start()

    def load_state(yb, carry):
        q_copy(yb).start()
        return carry

    lax.fori_loop(0, n_yb, load_state, 0)

    rows_all = q_ref.shape[1]
    n_rows = 16 * wx

    def clear_end(i, carry):
        at = pl.multiple_of(i * 8, 8)
        q_ref[0, pl.ds(at, 8), :] = jnp.zeros((8, BLK), F32)
        q_ref[n_yb + 1, pl.ds(at, 8), :] = jnp.zeros((8, BLK), F32)
        return carry

    lax.fori_loop(0, rows_all // 8, clear_end, 0)

    def clear_tail(yb, carry):
        q_ref[yb + 1, 0:pad, :] = jnp.zeros((pad, BLK), F32)
        tail = rows_all - (row_y + wx)
        q_ref[yb + 1, row_y + wx : rows_all, :] = jnp.zeros((tail, BLK), F32)
        return carry

    lax.fori_loop(0, n_yb, clear_tail, 0)
    anss[...] = jnp.zeros(anss.shape, F32)

    def clear_edge(yb, carry):
        for e in range(2):
            fe[e, yb] = jnp.zeros((16, BLK), F32)
        return carry

    lax.fori_loop(0, n_yb, clear_edge, 0)

    count = count_s[0]

    def places(i, carry):
        for g in range(8):
            t = i * 8 + g
            s = slot_s[t]
            a = (px + 1 - (s >> (bits_y + 1))) & (gx - 1)
            b = (py + 1 - (s >> 1)) & (gy - 1)
            at = jnp.minimum(a * 6 + b * 2 + (s & 1), n_blk - 1)
            at_s[t] = at
            loc_s[t] = jnp.where(t < count, at, jnp.int32(100))
            cell = cell_s[t]
            row_s[t] = ((cell & (n_yb - 1)) << bits_x) + (cell >> bits_b)
        return carry

    lax.fori_loop(0, n_tiles // 8, places, 0)

    for c in pay:
        c.wait_recv()
    for i in range(n_chunk):
        w_copy(i).wait()

    def gather(i):
        at = pl.multiple_of(i * group, group)
        for r in range(NQ):
            value = s_ref[pl.ds(r * pitch + at, group), :]
            c_ref[r // 2, pl.ds(at, group), (r % 2) * BLK : (r % 2 + 1) * BLK] = value.astype(BF16)

    def contrib(i, carry):
        gather(jnp.maximum(i - 1, 0))
        for g in range(0, group, 2):
            t = i * group + g
            left = jnp.concatenate([recv[at_s[t]], recv[at_s[t + 1]]], axis=0)
            right = jnp.concatenate([wts[t], wts[t + 1]], axis=1)
            c = jnp.dot(left, right, preferred_element_type=F32)
            s_ref[pl.ds(t, 16, stride=pitch), :] = c[0:16, 0:BLK]
            s_ref[pl.ds(t + 1, 16, stride=pitch), :] = c[16:32, BLK : 2 * BLK]
        return carry

    lax.fori_loop(0, n_tiles // group, contrib, 0)
    gather(n_tiles // group - 1)

    lane_t = lax.broadcasted_iota(jnp.int32, (1, n_tiles), 1)
    cell_m = jnp.broadcast_to(jnp.where(lane_t < count, cell_v[...], -1), (wx, n_tiles))
    cell_at = lax.broadcasted_iota(jnp.int32, (wx, n_tiles), 0) * n_yb

    def deposit(blocks):
        picks = []
        for yb in blocks:
            q_copy(yb).wait()
            picks.append(jnp.where(cell_m == cell_at + yb, 1.0, 0.0).astype(BF16))
        left = jnp.concatenate(picks, axis=0)
        mass = [jnp.ones((wx, BLK), F32) for _ in blocks]
        moving = [[] for _ in blocks]
        for p in range(NQ // 2):
            both = jnp.dot(left, c_ref[p], preferred_element_type=F32)
            for k, yb in enumerate(blocks):
                for h in range(2):
                    r = 2 * p + h
                    rows = pl.ds(pad + r * wx, wx)
                    value = (
                        q_ref[yb + 1, rows, :]
                        + both[k * wx : (k + 1) * wx, h * BLK : (h + 1) * BLK]
                    )
                    q_ref[yb + 1, rows, :] = value
                    if r < MAT:
                        mass[k] = mass[k] + dens[r] * value
                    elif r < MAT + 2:
                        moving[k].append(value)
        for k, yb in enumerate(blocks):
            scale = (0.5 * TIME_STEP) / mass[k]
            u = moving[k][0] * scale
            q_ref[yb + 1, pl.ds(row_x, wx), :] = u
            q_ref[yb + 1, pl.ds(row_y, wx), :] = moving[k][1] * scale
        for yb in blocks:
            for e, x in ((0, 0), (1, wx - 1)):
                edge = q_ref[yb + 1, pl.ds(pad + x, 16, stride=wx), :]
                xe[e, yb] = edge
                xs[e, yb] = edge.astype(BF16)

    deposit((0, n_yb - 1, 1, 2))

    lane = lax.broadcasted_iota(jnp.int32, (wx, BLK), 1)
    upper = lane >= NZ

    def rows_of(r):
        return pl.ds(pad + r * wx, wx)

    def pair(yb, p, top):
        if p < NQ // 2:
            one, two = q_ref[yb + 1, rows_of(2 * p), :], q_ref[yb + 1, rows_of(2 * p + 1), :]
        else:
            one = q_ref[yb + 1, pl.ds(row_y, wx), :]
            two = one
        turned = pltpu.roll(one, NZ, axis=1)
        return jnp.where(upper, two, turned) if top else jnp.where(upper, turned, two)

    for p in range(NQ // 2 + 1):
        ys[0, p] = pair(0, p, False).astype(BF16)
        ys[1, p] = pair(n_yb - 1, p, True).astype(BF16)
    halo = []
    for e, b in ((0, 0), (1, 2)):
        halo.append(
            pltpu.make_async_remote_copy(
                src_ref=ys.at[e], dst_ref=yr.at[1 - e], send_sem=hy_s.at[e], recv_sem=hy_r.at[1 - e],
                device_id=dev(1, b, 1), device_id_type=MESH,
            )
        )
        halo[-1].start()

    def deposit_inner(i, carry):
        deposit(tuple(4 * i + 3 + k for k in range(4)))
        return carry

    lax.fori_loop(0, n_yb // 4 - 1, deposit_inner, 0)

    for e, a in ((0, 0), (1, 2)):
        halo.append(
            pltpu.make_async_remote_copy(
                src_ref=xs.at[e], dst_ref=xr.at[1 - e], send_sem=hx_s.at[e], recv_sem=hx_r.at[1 - e],
                device_id=dev(a, 1, 1), device_id_type=MESH,
            )
        )
        halo[-1].start()

    parts = 2
    half = wx // parts
    sub = lax.broadcasted_iota(jnp.int32, (half, BLK), 0)
    lane_h = lax.broadcasted_iota(jnp.int32, (half, BLK), 1)
    upper_h = lane_h >= NZ

    def remap(yb, carry):
        lanes = pl.ds(pl.multiple_of(yb * BLK, BLK), BLK)
        for part in range(parts):
            x0 = part * half

            def at(base, shift=0):
                return pl.ds(base + x0 + shift, half)

            ux = q_ref[yb + 1, at(row_x), :]
            lo = q_ref[yb + 1, at(row_x, -1), :] + ux
            hi = ux + q_ref[yb + 1, at(row_x, 1), :]
            if part == 0:
                lo = jnp.where(sub == 0, 0.0, lo)
            elif part == parts - 1:
                hi = jnp.where(sub == half - 1, 0.0, hi)
            uy = q_ref[yb + 1, at(row_y), :]
            prev, after = q_ref[yb, at(row_y), :], q_ref[yb + 2, at(row_y), :]
            y_hi = uy + pltpu.roll(jnp.where(upper_h, uy, after), NZ, axis=1)
            y_lo = uy + pltpu.roll(jnp.where(upper_h, prev, uy), NZ, axis=1)
            place = lane_h + yb * BLK
            y_lo = jnp.where(place < NZ, 0.0, y_lo)
            y_hi = jnp.where(place >= n_yb * BLK - NZ, 0.0, y_hi)
            c_xm = jnp.maximum(lo, 0.0)
            c_xp = -jnp.minimum(hi, 0.0)
            c_ym = jnp.maximum(y_lo, 0.0)
            c_yp = -jnp.minimum(y_hi, 0.0)
            c_0 = (1.0 - jnp.maximum(hi, 0.0) + jnp.minimum(lo, 0.0)) - (
                jnp.maximum(y_hi, 0.0) - jnp.minimum(y_lo, 0.0)
            )
            t_p = pltpu.roll(c_yp, NZ, axis=1)
            t_m = pltpu.roll(c_ym, NZ, axis=1)
            own = jnp.where(upper_h, t_p, t_m)
            other = jnp.where(upper_h, t_m, t_p)
            acc = jnp.zeros((half, BLK), F32)
            for r in range(NQ):
                base = pad + r * wx
                q = q_ref[yb + 1, at(base), :]
                beside = jnp.where(upper_h, q_ref[yb, at(base), :], q_ref[yb + 2, at(base), :])
                fresh = (
                    c_0 * q
                    + c_xm * q_ref[yb + 1, at(base, -1), :]
                    + c_xp * q_ref[yb + 1, at(base, 1), :]
                    + pltpu.roll(own * q + other * beside, NZ, axis=1)
                )
                f_ref[pl.ds(r * wx + x0, half), lanes] = fresh
                if part == 0:
                    fe[0, yb, r : r + 1, :] = fresh[0:1]
                elif part == parts - 1:
                    fe[1, yb, r : r + 1, :] = fresh[half - 1 : half]
                if r < MAT:
                    acc = acc + fresh * (stiff[r] + (0.5 * stiff[r]) * fresh)
                elif r == NQ - 1:
                    acc = acc + 0.4 * fresh
            press[pl.ds(pl.multiple_of(yb * wx + x0, half), half), :] = acc.astype(BF16).astype(F32)
        return carry

    lax.fori_loop(0, n_yb, remap, 0)

    for c in halo[:2]:
        c.wait_recv()
    has = [
        jnp.where(py > 0, 1.0, 0.0).astype(F32),
        jnp.where(py < gy - 1, 1.0, 0.0).astype(F32),
    ]
    for e, yb in ((0, 0), (1, n_yb - 1)):
        inside = jnp.logical_not(upper) if e == 0 else upper
        speed = q_ref[yb + 1, pl.ds(row_y, wx), :] + has[e] * yr[e, NQ // 2].astype(F32)
        speed = jnp.where(inside, speed, 0.0)
        pos, neg = jnp.maximum(speed, 0.0), jnp.minimum(speed, 0.0)
        w_far, w_own = (has[e] * pos, neg) if e == 0 else (-has[e] * neg, -pos)
        acc = jnp.zeros((wx, BLK), F32)
        for p in range(NQ // 2):
            packed = yr[e, p].astype(F32)
            for h in range(2):
                r = 2 * p + h
                far = packed if h == 0 else pltpu.roll(packed, NZ, axis=1)
                here = (slice(r * wx, (r + 1) * wx), slice(yb * BLK, (yb + 1) * BLK))
                fresh = f_ref[here] + (w_far * far + w_own * q_ref[yb + 1, rows_of(r), :])
                f_ref[here] = fresh
                fe[0, yb, r : r + 1, :] = fresh[0:1]
                fe[1, yb, r : r + 1, :] = fresh[wx - 1 : wx]
                if r < MAT:
                    acc = acc + fresh * (stiff[r] + (0.5 * stiff[r]) * fresh)
                elif r == NQ - 1:
                    acc = acc + 0.4 * fresh
        press[yb * wx : (yb + 1) * wx, :] = acc.astype(BF16).astype(F32)

    for c in halo[2:]:
        c.wait_recv()
    sub16 = lax.broadcasted_iota(jnp.int32, (16, BLK), 0)
    lin = jnp.zeros((16, BLK), F32)
    for m in range(MAT):
        lin = jnp.where(sub16 == m, stiff[m], lin)
    quad = 0.5 * lin
    lin = jnp.where(sub16 == NQ - 1, 0.4, lin)
    has = [
        jnp.where(px > 0, 1.0, 0.0).astype(F32),
        jnp.where(px < gx - 1, 1.0, 0.0).astype(F32),
    ]

    def border_x(i, carry):
        for yb in (2 * i, 2 * i + 1):
            lanes = pl.ds(pl.multiple_of(yb * BLK, BLK), BLK)
            for e, x in ((0, 0), (1, wx - 1)):
                far = xr[e, yb].astype(F32) * has[e]
                q = xe[e, yb]
                speed = q[NQ : NQ + 1] + far[NQ : NQ + 1]
                pos, neg = jnp.maximum(speed, 0.0), jnp.minimum(speed, 0.0)
                change = (pos * far + neg * q) if e == 0 else -(pos * q + neg * far)
                fresh = fe[e, yb] + change
                for r in range(NQ):
                    f_ref[r * wx + x : r * wx + x + 1, lanes] = fresh[r : r + 1]
                terms = jnp.where(sub16 < NQ, fresh * (lin + quad * fresh), 0.0)
                value = jnp.sum(terms, axis=0, keepdims=True)
                press[pl.ds(yb * wx + x, 1), :] = value.astype(BF16).astype(F32)
        return carry

    lax.fori_loop(0, n_yb // 2, border_x, 0)

    sub24 = lax.broadcasted_iota(jnp.int32, (24, BLK), 0)

    many = 2 * group

    def sample(i, acc):
        lefts, rights = [], []
        for g in range(many):
            t = i * many + g
            hit = sub24 == loc_s[t]
            value = jnp.broadcast_to(press[pl.ds(row_s[t], 1), :], (24, BLK))
            lefts.append(
                jnp.concatenate(
                    [jnp.where(hit, value, 0.0), jnp.where(hit, 1.0, 0.0)], axis=0
                ).astype(BF16)
            )
            rights.append(wts[t])
        return acc + lax.dot_general(
            jnp.concatenate(lefts, axis=1), jnp.concatenate(rights, axis=1),
            (((1,), (1,)), ((), ())), preferred_element_type=F32,
        )

    acc = lax.fori_loop(0, n_tiles // many, sample, jnp.zeros((48, BLK), F32))
    answer = (acc[0:24] / jnp.maximum(acc[24:48], 1.0)).astype(BF16).astype(F32)

    back = []
    for n, (a, b) in enumerate(NEAR):
        rows = slice(8 * n, 8 * n + 2)
        if n == OWN:
            ret[rows, :] = answer[2 * n : 2 * n + 2]
        else:
            anss[rows, :] = answer[2 * n : 2 * n + 2]
    for n, (a, b) in enumerate(NEAR):
        if n != OWN:
            i = len(back)
            back.append(
                pltpu.make_async_remote_copy(
                    src_ref=anss.at[pl.ds(8 * n, 8)], dst_ref=ret.at[pl.ds(8 * n, 8)],
                    send_sem=ret_s.at[i], recv_sem=ret_r.at[i],
                    device_id=dev(a, b, -1), device_id_type=MESH,
                )
            )
            back[-1].start()
    sub32 = lax.broadcasted_iota(jnp.int32, (32, BLK), 0)
    lane32 = lax.broadcasted_iota(jnp.int32, (32, BLK), 1)
    wanted = jnp.full((32, BLK), -1, jnp.int32)
    for n in range(9):
        wanted = jnp.where(sub32 == first[n], 8 * n, wanted)
        wanted = jnp.where(sub32 == second[n], 8 * n + 1, wanted)
    mine = jnp.where(wanted == lane32, 1.0, 0.0).astype(BF16)
    for c in pay + halo:
        c.wait_send()
    for c in back:
        c.wait_recv()
    result = jnp.dot(mine, ret[...].astype(BF16), preferred_element_type=F32)
    eo_ref[...] = result[0:n_blk]
    for c in back:
        c.wait_send()


def write_out(f_ref, eo_ref, out_ref, ep_ref, sem):
    step = f_ref.shape[0] // sem.shape[0]
    copies = [
        pltpu.make_async_copy(f_ref.at[pl.ds(i * step, step)], out_ref.at[pl.ds(i * step, step)], sem.at[i])
        for i in range(sem.shape[0])
    ]
    for c in copies:
        c.start()
    ep_ref[...] = eo_ref[...].astype(BF16)
    for c in copies:
        c.wait()


def per_device(
    elem_volume, elem_velocity, elem_energy, elem_mat, elem_dest, tile_slot, tile_cell,
    tile_weight, tile_count, cell_state, mat_props,
):
    gx, gy = lax.axis_size("gx"), lax.axis_size("gy")
    n_blk = elem_dest.shape[0]
    n_tiles = tile_weight.shape[0]
    wx, lanes = cell_state.shape[1], cell_state.shape[2]
    n_yb = lanes // BLK
    rows_q = 16 * wx + 16
    vmem = pl.BlockSpec(memory_space=pltpu.VMEM)
    smem, i32 = pltpu.SMEM, jnp.int32
    hbm = pl.BlockSpec(memory_space=pltpu.HBM)
    dma = pltpu.SemaphoreType.DMA
    fresh, eo = pl.pallas_call(
        functools.partial(kernel, (gx, gy, n_blk, n_tiles, wx, n_yb)),
        out_shape=(
            pltpu.VMEM((NQ * wx, lanes), F32),
            pltpu.VMEM((n_blk, BLK), F32),
        ),
        in_specs=[hbm] * 12,
        out_specs=(vmem, vmem),
        scratch_shapes=[
            pltpu.VMEM((n_blk, BLK), F32), pltpu.VMEM((3, n_blk * BLK), F32),
            pltpu.VMEM((n_blk, BLK), F32), pltpu.VMEM((n_blk, BLK), i32), pltpu.VMEM((1, n_tiles), i32),
            smem((n_blk,), i32), smem((n_tiles,), i32), smem((n_tiles,), i32), smem((1,), i32), smem((2, MAT), F32),
            pltpu.VMEM((n_tiles, BLK, BLK), BF16),
            pltpu.VMEM((n_yb + 2, rows_q, BLK), F32),
            pltpu.VMEM((2, n_yb, 16, BLK), F32),
            pltpu.VMEM((2, n_yb, 16, BLK), F32),
            smem((n_tiles,), i32), smem((n_tiles,), i32), smem((n_tiles,), i32),
            pltpu.VMEM((16 * n_tiles + 24, BLK), F32),
            pltpu.VMEM((NQ // 2, n_tiles, 2 * BLK), BF16),
            pltpu.VMEM((n_yb * wx, BLK), F32),
            pltpu.VMEM((n_blk, 16, BLK), F32),
            pltpu.VMEM((n_blk, 16, BLK), BF16),
            pltpu.VMEM((n_blk, 16, BLK), BF16),
            pltpu.VMEM((2, n_yb, 16, BLK), BF16),
            pltpu.VMEM((2, n_yb, 16, BLK), BF16),
            pltpu.VMEM((2, NQ // 2 + 1, wx, BLK), BF16),
            pltpu.VMEM((2, NQ // 2 + 1, wx, BLK), BF16),
            pltpu.VMEM((128, BLK), F32),
            pltpu.VMEM((128, BLK), F32),
            dma((10,)), dma((4,)), dma((n_yb,)),
            dma((8,)), dma((8,)), dma((2,)), dma((2,)), dma((2,)), dma((2,)), dma((8,)), dma((8,)),
        ],
        compiler_params=pltpu.CompilerParams(
            collective_id=0, has_side_effects=True, vmem_limit_bytes=67043328 - 6291456 - 16384
        ),
    )(
        elem_volume.reshape(n_blk, BLK), elem_velocity, elem_energy.reshape(n_blk, BLK),
        elem_mat.reshape(n_blk, BLK), tile_cell.reshape(1, n_tiles),
        elem_dest, tile_slot, tile_cell, tile_count, mat_props,
        tile_weight, cell_state.reshape(NQ * wx, lanes),
    )
    out, pressure = pl.pallas_call(
        write_out,
        out_shape=(
            jax.ShapeDtypeStruct((NQ * wx, lanes), F32),
            jax.ShapeDtypeStruct((n_blk, BLK), BF16),
        ),
        in_specs=[vmem, vmem],
        out_specs=(hbm, vmem),
        scratch_shapes=[dma((8,))],
        compiler_params=pltpu.CompilerParams(vmem_limit_bytes=4 * 1024 * 1024),
    )(fresh, eo)
    return out.reshape(NQ, wx, lanes), pressure.reshape(n_blk * BLK)


def solution(mesh):
    both = ("gx", "gy")
    return jax.shard_map(
        per_device,
        mesh=mesh,
        in_specs=(
            P(both), P(None, both), P(both), P(both), P(both), P(both), P(both),
            P(both, None, None), P(both), P(None, "gx", "gy"), P(),
        ),
        out_specs=(P(None, "gx", "gy"), P(both)),
        check_vma=False,
    )
```

```python
import functools

import jax
import jax.numpy as jnp
from jax import lax
from jax.experimental import pallas as pl
from jax.experimental.pallas import tpu as pltpu
from jax.sharding import PartitionSpec as P

MAT = 8
NQ = 12
NZ = 64
BLK = 128
CAP = 2
TIME_STEP = 0.8
NEAR = [(a, b) for a in range(3) for b in range(3)]
OWN = 4
F32 = jnp.float32
BF16 = jnp.bfloat16
MESH = pl.DeviceIdType.MESH


def kernel(
    dims,
    vol_h, vel_h, ene_h, mat_h, cell_h, dest_h, slot_h, cell1_h, count_h, props_h, w_hbm, state_hbm,
    f_ref, eo_ref,
    vol, vel, ene, mat, cell_v, dest_s, slot_s, cell_s, count_s, props_s,
    wts, q_ref, xe, fe, at_s, loc_s, row_s, s_ref, c_ref, press, blk, outg, recv, xs, xr, ys, yr, anss, ret,
    in_sem, w_sem, q_sem, pay_s, pay_r, hx_s, hx_r, hy_s, hy_r, ret_s, ret_r,
):
    gx, gy, n_blk, n_tiles, wx, n_yb = dims
    px = lax.axis_index("gx")
    py = lax.axis_index("gy")
    group = 16
    pitch = n_tiles + 1
    bits_y, bits_b, bits_x = gy.bit_length() - 1, n_yb.bit_length() - 1, wx.bit_length() - 1
    assert (gx & (gx - 1), gy, n_yb, wx, CAP) == (0, 1 << bits_y, 1 << bits_b, 1 << bits_x, 2)
    n_chunk = 4
    tiles_chunk = n_tiles // n_chunk
    pad = 8
    row_x = pad + NQ * wx
    row_y = row_x + wx

    def dev(a, b, sign):
        return (lax.rem(px + sign * (a - 1) + gx, gx), lax.rem(py + sign * (b - 1) + gy, gy))

    def w_copy(i):
        part = pl.ds(i * tiles_chunk, tiles_chunk)
        return pltpu.make_async_copy(w_hbm.at[part], wts.at[part], w_sem.at[i])

    def q_copy(yb):
        return pltpu.make_async_copy(
            state_hbm.at[:, pl.ds(yb * BLK, BLK)],
            q_ref.at[yb + 1, pl.ds(pad, NQ * wx)],
            q_sem.at[yb],
        )

    ret[...] = jnp.zeros(ret.shape, F32)
    barrier = pltpu.get_barrier_semaphore()
    for a, b in NEAR:
        if (a, b) != (1, 1):
            pl.semaphore_signal(barrier, inc=1, device_id=dev(a, b, 1), device_id_type=MESH)
    small = [
        pltpu.make_async_copy(src, dst, in_sem.at[i])
        for i, (src, dst) in enumerate((
            (dest_h, dest_s), (props_h, props_s), (vol_h, vol), (mat_h, mat), (vel_h, vel),
            (ene_h, ene), (slot_h, slot_s), (cell1_h, cell_s), (count_h, count_s), (cell_h, cell_v),
        ))
    ]
    for c in small:
        c.start()
    for c in small[:6]:
        c.wait()
    for i in range(n_chunk):
        w_copy(i).start()

    sub8 = lax.broadcasted_iota(jnp.int32, (8, BLK), 0)
    dens = [props_s[0, m] for m in range(MAT)]
    stiff = [props_s[1, m] for m in range(MAT)]
    dens_col = jnp.zeros((8, BLK), F32)
    for m in range(MAT):
        dens_col = jnp.where(sub8 == m, dens[m], dens_col)
    blk[...] = jnp.zeros(blk.shape, F32)
    for j in range(n_blk):
        hit = jnp.broadcast_to(mat[j : j + 1, :], (8, BLK)) == sub8
        v = vol[j : j + 1, :]
        blk[j, 0:8, :] = jnp.where(hit, jnp.broadcast_to(v, (8, BLK)), 0.0)
        mass = v * jnp.sum(jnp.where(hit, dens_col, 0.0), axis=0, keepdims=True)
        blk[j, 8:11, :] = mass * vel[:, j * BLK : (j + 1) * BLK]
        blk[j, 11:12, :] = mass * ene[j : j + 1, :]
    first, second = [], []
    keys = []
    for j in range(n_blk):
        d = dest_s[j]
        ka = ((d >> bits_y) - px + 1) & (gx - 1)
        kb = (d - py + 1) & (gy - 1)
        keys.append(ka * 3 + kb)
    for n in range(9):
        low = jnp.int32(0)
        total = jnp.int32(0)
        for j in reversed(range(n_blk)):
            same = keys[j] == n
            low = jnp.where(same, jnp.int32(j), low)
            total = total + jnp.where(same, jnp.int32(j), jnp.int32(0))
        first.append(low)
        second.append(jnp.minimum(total - low, n_blk - 1))
    for n in range(9):
        for rank, src in ((0, first[n]), (1, second[n])):
            value = blk[src].astype(BF16)
            if n == OWN:
                recv[2 * n + rank] = value
            else:
                outg[2 * n + rank] = value

    pl.semaphore_wait(barrier, 8)
    pay = []
    for n, (a, b) in enumerate(NEAR):
        if n != OWN:
            i = len(pay)
            pay.append(
                pltpu.make_async_remote_copy(
                    src_ref=outg.at[pl.ds(2 * n, 2)], dst_ref=recv.at[pl.ds(2 * n, 2)],
                    send_sem=pay_s.at[i], recv_sem=pay_r.at[i],
                    device_id=dev(a, b, 1), device_id_type=MESH,
                )
            )
            pay[-1].start()

    def load_state(yb, carry):
        q_copy(yb).start()
        return carry

    lax.fori_loop(0, n_yb, load_state, 0)

    rows_all = q_ref.shape[1]
    n_rows = 16 * wx

    def clear_end(i, carry):
        at = pl.multiple_of(i * 8, 8)
        q_ref[0, pl.ds(at, 8), :] = jnp.zeros((8, BLK), F32)
        q_ref[n_yb + 1, pl.ds(at, 8), :] = jnp.zeros((8, BLK), F32)
        return carry

    lax.fori_loop(0, rows_all // 8, clear_end, 0)

    def clear_tail(yb, carry):
        q_ref[yb + 1, 0:pad, :] = jnp.zeros((pad, BLK), F32)
        tail = rows_all - (row_y + wx)
        q_ref[yb + 1, row_y + wx : rows_all, :] = jnp.zeros((tail, BLK), F32)
        return carry

    lax.fori_loop(0, n_yb, clear_tail, 0)
    anss[...] = jnp.zeros(anss.shape, F32)

    def clear_edge(yb, carry):
        for e in range(2):
            fe[e, yb] = jnp.zeros((16, BLK), F32)
        return carry

    lax.fori_loop(0, n_yb, clear_edge, 0)

    for c in small[6:]:
        c.wait()
    count = count_s[0]

    def places(i, carry):
        for g in range(8):
            t = i * 8 + g
            s = slot_s[t]
            a = (px + 1 - (s >> (bits_y + 1))) & (gx - 1)
            b = (py + 1 - (s >> 1)) & (gy - 1)
            at = jnp.minimum(a * 6 + b * 2 + (s & 1), n_blk - 1)
            at_s[t] = at
            loc_s[t] = jnp.where(t < count, at, jnp.int32(100))
            cell = cell_s[t]
            row_s[t] = ((cell & (n_yb - 1)) << bits_x) + (cell >> bits_b)
        return carry

    lax.fori_loop(0, n_tiles // 8, places, 0)

    for c in pay:
        c.wait_recv()
    for i in range(n_chunk):
        w_copy(i).wait()

    def gather(i):
        at = pl.multiple_of(i * group, group)
        for r in range(NQ):
            value = s_ref[pl.ds(r * pitch + at, group), :]
            c_ref[r // 2, pl.ds(at, group), (r % 2) * BLK : (r % 2 + 1) * BLK] = value.astype(BF16)

    def contrib(i, carry):
        gather(jnp.maximum(i - 1, 0))
        for g in range(0, group, 2):
            t = i * group + g
            left = jnp.concatenate([recv[at_s[t]], recv[at_s[t + 1]]], axis=0)
            right = jnp.concatenate([wts[t], wts[t + 1]], axis=1)
            c = jnp.dot(left, right, preferred_element_type=F32)
            s_ref[pl.ds(t, 16, stride=pitch), :] = c[0:16, 0:BLK]
            s_ref[pl.ds(t + 1, 16, stride=pitch), :] = c[16:32, BLK : 2 * BLK]
        return carry

    lax.fori_loop(0, n_tiles // group, contrib, 0)
    gather(n_tiles // group - 1)

    lane_t = lax.broadcasted_iota(jnp.int32, (1, n_tiles), 1)
    cell_m = jnp.broadcast_to(jnp.where(lane_t < count, cell_v[...], -1), (wx, n_tiles))
    cell_at = lax.broadcasted_iota(jnp.int32, (wx, n_tiles), 0) * n_yb

    def deposit(blocks):
        picks = []
        for yb in blocks:
            q_copy(yb).wait()
            picks.append(jnp.where(cell_m == cell_at + yb, 1.0, 0.0).astype(BF16))
        left = jnp.concatenate(picks, axis=0)
        mass = [jnp.ones((wx, BLK), F32) for _ in blocks]
        moving = [[] for _ in blocks]
        for p in range(NQ // 2):
            both = jnp.dot(left, c_ref[p], preferred_element_type=F32)
            for k, yb in enumerate(blocks):
                for h in range(2):
                    r = 2 * p + h
                    rows = pl.ds(pad + r * wx, wx)
                    value = (
                        q_ref[yb + 1, rows, :]
                        + both[k * wx : (k + 1) * wx, h * BLK : (h + 1) * BLK]
                    )
                    q_ref[yb + 1, rows, :] = value
                    if r < MAT:
                        mass[k] = mass[k] + dens[r] * value
                    elif r < MAT + 2:
                        moving[k].append(value)
        for k, yb in enumerate(blocks):
            scale = (0.5 * TIME_STEP) / mass[k]
            u = moving[k][0] * scale
            q_ref[yb + 1, pl.ds(row_x, wx), :] = u
            q_ref[yb + 1, pl.ds(row_y, wx), :] = moving[k][1] * scale
        for yb in blocks:
            for e, x in ((0, 0), (1, wx - 1)):
                edge = q_ref[yb + 1, pl.ds(pad + x, 16, stride=wx), :]
                xe[e, yb] = edge
                xs[e, yb] = edge.astype(BF16)

    deposit((0, n_yb - 1, 1, 2))

    lane = lax.broadcasted_iota(jnp.int32, (wx, BLK), 1)
    upper = lane >= NZ

    def rows_of(r):
        return pl.ds(pad + r * wx, wx)

    def pair(yb, p, top):
        if p < NQ // 2:
            one, two = q_ref[yb + 1, rows_of(2 * p), :], q_ref[yb + 1, rows_of(2 * p + 1), :]
        else:
            one = q_ref[yb + 1, pl.ds(row_y, wx), :]
            two = one
        turned = pltpu.roll(one, NZ, axis=1)
        return jnp.where(upper, two, turned) if top else jnp.where(upper, turned, two)

    for p in range(NQ // 2 + 1):
        ys[0, p] = pair(0, p, False).astype(BF16)
        ys[1, p] = pair(n_yb - 1, p, True).astype(BF16)
    halo = []
    for e, b in ((0, 0), (1, 2)):
        halo.append(
            pltpu.make_async_remote_copy(
                src_ref=ys.at[e], dst_ref=yr.at[1 - e], send_sem=hy_s.at[e], recv_sem=hy_r.at[1 - e],
                device_id=dev(1, b, 1), device_id_type=MESH,
            )
        )
        halo[-1].start()

    def deposit_inner(i, carry):
        deposit(tuple(4 * i + 3 + k for k in range(4)))
        return carry

    lax.fori_loop(0, n_yb // 4 - 1, deposit_inner, 0)

    for e, a in ((0, 0), (1, 2)):
        halo.append(
            pltpu.make_async_remote_copy(
                src_ref=xs.at[e], dst_ref=xr.at[1 - e], send_sem=hx_s.at[e], recv_sem=hx_r.at[1 - e],
                device_id=dev(a, 1, 1), device_id_type=MESH,
            )
        )
        halo[-1].start()

    parts = 2
    half = wx // parts
    sub = lax.broadcasted_iota(jnp.int32, (half, BLK), 0)
    lane_h = lax.broadcasted_iota(jnp.int32, (half, BLK), 1)

    def remap(yb, carry):
        lanes = pl.ds(pl.multiple_of(yb * BLK, BLK), BLK)
        upper_h = lane_h >= NZ + jnp.minimum(yb, 0)
        for part in range(parts):
            x0 = part * half

            def at(base, shift=0):
                return pl.ds(base + x0 + shift, half)

            ux = q_ref[yb + 1, at(row_x), :]
            lo = q_ref[yb + 1, at(row_x, -1), :] + ux
            hi = ux + q_ref[yb + 1, at(row_x, 1), :]
            if part == 0:
                lo = jnp.where(sub == 0, 0.0, lo)
            elif part == parts - 1:
                hi = jnp.where(sub == half - 1, 0.0, hi)
            uy = q_ref[yb + 1, at(row_y), :]
            prev, after = q_ref[yb, at(row_y), :], q_ref[yb + 2, at(row_y), :]
            y_hi = uy + pltpu.roll(jnp.where(upper_h, uy, after), NZ, axis=1)
            y_lo = uy + pltpu.roll(jnp.where(upper_h, prev, uy), NZ, axis=1)
            place = lane_h + yb * BLK
            y_lo = jnp.where(place < NZ, 0.0, y_lo)
            y_hi = jnp.where(place >= n_yb * BLK - NZ, 0.0, y_hi)
            c_xm = jnp.maximum(lo, 0.0)
            c_xp = -jnp.minimum(hi, 0.0)
            c_ym = jnp.maximum(y_lo, 0.0)
            c_yp = -jnp.minimum(y_hi, 0.0)
            c_0 = (1.0 - jnp.maximum(hi, 0.0) + jnp.minimum(lo, 0.0)) - (
                jnp.maximum(y_hi, 0.0) - jnp.minimum(y_lo, 0.0)
            )
            t_p = pltpu.roll(c_yp, NZ, axis=1)
            t_m = pltpu.roll(c_ym, NZ, axis=1)
            own = jnp.where(upper_h, t_p, t_m)
            other = jnp.where(upper_h, t_m, t_p)
            acc = jnp.zeros((half, BLK), F32)
            for r in range(NQ):
                base = pad + r * wx
                q = q_ref[yb + 1, at(base), :]
                beside = jnp.where(upper_h, q_ref[yb, at(base), :], q_ref[yb + 2, at(base), :])
                fresh = (
                    c_0 * q
                    + c_xm * q_ref[yb + 1, at(base, -1), :]
                    + c_xp * q_ref[yb + 1, at(base, 1), :]
                    + pltpu.roll(own * q + other * beside, NZ, axis=1)
                )
                f_ref[pl.ds(r * wx + x0, half), lanes] = fresh
                if part == 0:
                    fe[0, yb, r : r + 1, :] = fresh[0:1]
                elif part == parts - 1:
                    fe[1, yb, r : r + 1, :] = fresh[half - 1 : half]
                if r < MAT:
                    acc = acc + fresh * (stiff[r] + (0.5 * stiff[r]) * fresh)
                elif r == NQ - 1:
                    acc = acc + 0.4 * fresh
            press[pl.ds(pl.multiple_of(yb * wx + x0, half), half), :] = acc.astype(BF16).astype(F32)
        return carry

    lax.fori_loop(0, n_yb, remap, 0)

    for c in halo[:2]:
        c.wait_recv()
    has = [
        jnp.where(py > 0, 1.0, 0.0).astype(F32),
        jnp.where(py < gy - 1, 1.0, 0.0).astype(F32),
    ]
    for e, yb in ((0, 0), (1, n_yb - 1)):
        inside = jnp.logical_not(upper) if e == 0 else upper
        speed = q_ref[yb + 1, pl.ds(row_y, wx), :] + has[e] * yr[e, NQ // 2].astype(F32)
        speed = jnp.where(inside, speed, 0.0)
        pos, neg = jnp.maximum(speed, 0.0), jnp.minimum(speed, 0.0)
        w_far, w_own = (has[e] * pos, neg) if e == 0 else (-has[e] * neg, -pos)
        acc = jnp.zeros((wx, BLK), F32)
        for p in range(NQ // 2):
            packed = yr[e, p].astype(F32)
            for h in range(2):
                r = 2 * p + h
                far = packed if h == 0 else pltpu.roll(packed, NZ, axis=1)
                here = (slice(r * wx, (r + 1) * wx), slice(yb * BLK, (yb + 1) * BLK))
                fresh = f_ref[here] + (w_far * far + w_own * q_ref[yb + 1, rows_of(r), :])
                f_ref[here] = fresh
                fe[0, yb, r : r + 1, :] = fresh[0:1]
                fe[1, yb, r : r + 1, :] = fresh[wx - 1 : wx]
                if r < MAT:
                    acc = acc + fresh * (stiff[r] + (0.5 * stiff[r]) * fresh)
                elif r == NQ - 1:
                    acc = acc + 0.4 * fresh
        press[yb * wx : (yb + 1) * wx, :] = acc.astype(BF16).astype(F32)

    for c in halo[2:]:
        c.wait_recv()
    sub16 = lax.broadcasted_iota(jnp.int32, (16, BLK), 0)
    lin = jnp.zeros((16, BLK), F32)
    for m in range(MAT):
        lin = jnp.where(sub16 == m, stiff[m], lin)
    quad = 0.5 * lin
    lin = jnp.where(sub16 == NQ - 1, 0.4, lin)
    has = [
        jnp.where(px > 0, 1.0, 0.0).astype(F32),
        jnp.where(px < gx - 1, 1.0, 0.0).astype(F32),
    ]

    def border_x(i, carry):
        for yb in (2 * i, 2 * i + 1):
            lanes = pl.ds(pl.multiple_of(yb * BLK, BLK), BLK)
            for e, x in ((0, 0), (1, wx - 1)):
                far = xr[e, yb].astype(F32) * has[e]
                q = xe[e, yb]
                speed = q[NQ : NQ + 1] + far[NQ : NQ + 1]
                pos, neg = jnp.maximum(speed, 0.0), jnp.minimum(speed, 0.0)
                change = (pos * far + neg * q) if e == 0 else -(pos * q + neg * far)
                fresh = fe[e, yb] + change
                for r in range(NQ):
                    f_ref[r * wx + x : r * wx + x + 1, lanes] = fresh[r : r + 1]
                terms = jnp.where(sub16 < NQ, fresh * (lin + quad * fresh), 0.0)
                value = jnp.sum(terms, axis=0, keepdims=True)
                press[pl.ds(yb * wx + x, 1), :] = value.astype(BF16).astype(F32)
        return carry

    lax.fori_loop(0, n_yb // 2, border_x, 0)

    sub24 = lax.broadcasted_iota(jnp.int32, (24, BLK), 0)

    many = 2 * group

    def sample(i, acc):
        lefts, rights = [], []
        for g in range(many):
            t = i * many + g
            hit = sub24 == loc_s[t]
            value = jnp.broadcast_to(press[pl.ds(row_s[t], 1), :], (24, BLK))
            lefts.append(
                jnp.concatenate(
                    [jnp.where(hit, value, 0.0), jnp.where(hit, 1.0, 0.0)], axis=0
                ).astype(BF16)
            )
            rights.append(wts[t])
        return acc + lax.dot_general(
            jnp.concatenate(lefts, axis=1), jnp.concatenate(rights, axis=1),
            (((1,), (1,)), ((), ())), preferred_element_type=F32,
        )

    acc = lax.fori_loop(0, n_tiles // many, sample, jnp.zeros((48, BLK), F32))
    answer = (acc[0:24] / jnp.maximum(acc[24:48], 1.0)).astype(BF16).astype(F32)

    back = []
    for n, (a, b) in enumerate(NEAR):
        rows = slice(8 * n, 8 * n + 2)
        if n == OWN:
            ret[rows, :] = answer[2 * n : 2 * n + 2]
        else:
            anss[rows, :] = answer[2 * n : 2 * n + 2]
    for n, (a, b) in enumerate(NEAR):
        if n != OWN:
            i = len(back)
            back.append(
                pltpu.make_async_remote_copy(
                    src_ref=anss.at[pl.ds(8 * n, 8)], dst_ref=ret.at[pl.ds(8 * n, 8)],
                    send_sem=ret_s.at[i], recv_sem=ret_r.at[i],
                    device_id=dev(a, b, -1), device_id_type=MESH,
                )
            )
            back[-1].start()
    sub32 = lax.broadcasted_iota(jnp.int32, (32, BLK), 0)
    lane32 = lax.broadcasted_iota(jnp.int32, (32, BLK), 1)
    wanted = jnp.full((32, BLK), -1, jnp.int32)
    for n in range(9):
        wanted = jnp.where(sub32 == first[n], 8 * n, wanted)
        wanted = jnp.where(sub32 == second[n], 8 * n + 1, wanted)
    mine = jnp.where(wanted == lane32, 1.0, 0.0).astype(BF16)
    for c in pay + halo:
        c.wait_send()
    for c in back:
        c.wait_recv()
    result = jnp.dot(mine, ret[...].astype(BF16), preferred_element_type=F32)
    eo_ref[...] = result[0:n_blk]
    for c in back:
        c.wait_send()


def write_out(f_ref, eo_ref, out_ref, ep_ref, sem):
    step = f_ref.shape[0] // sem.shape[0]
    copies = [
        pltpu.make_async_copy(f_ref.at[pl.ds(i * step, step)], out_ref.at[pl.ds(i * step, step)], sem.at[i])
        for i in range(sem.shape[0])
    ]
    for c in copies:
        c.start()
    ep_ref[...] = eo_ref[...].astype(BF16)
    for c in copies:
        c.wait()


def per_device(
    elem_volume, elem_velocity, elem_energy, elem_mat, elem_dest, tile_slot, tile_cell,
    tile_weight, tile_count, cell_state, mat_props,
):
    gx, gy = lax.axis_size("gx"), lax.axis_size("gy")
    n_blk = elem_dest.shape[0]
    n_tiles = tile_weight.shape[0]
    wx, lanes = cell_state.shape[1], cell_state.shape[2]
    n_yb = lanes // BLK
    rows_q = 16 * wx + 16
    vmem = pl.BlockSpec(memory_space=pltpu.VMEM)
    smem, i32 = pltpu.SMEM, jnp.int32
    hbm = pl.BlockSpec(memory_space=pltpu.HBM)
    dma = pltpu.SemaphoreType.DMA
    fresh, eo = pl.pallas_call(
        functools.partial(kernel, (gx, gy, n_blk, n_tiles, wx, n_yb)),
        out_shape=(
            pltpu.VMEM((NQ * wx, lanes), F32),
            pltpu.VMEM((n_blk, BLK), F32),
        ),
        in_specs=[hbm] * 12,
        out_specs=(vmem, vmem),
        scratch_shapes=[
            pltpu.VMEM((n_blk, BLK), F32), pltpu.VMEM((3, n_blk * BLK), F32),
            pltpu.VMEM((n_blk, BLK), F32), pltpu.VMEM((n_blk, BLK), i32), pltpu.VMEM((1, n_tiles), i32),
            smem((n_blk,), i32), smem((n_tiles,), i32), smem((n_tiles,), i32), smem((1,), i32), smem((2, MAT), F32),
            pltpu.VMEM((n_tiles, BLK, BLK), BF16),
            pltpu.VMEM((n_yb + 2, rows_q, BLK), F32),
            pltpu.VMEM((2, n_yb, 16, BLK), F32),
            pltpu.VMEM((2, n_yb, 16, BLK), F32),
            smem((n_tiles,), i32), smem((n_tiles,), i32), smem((n_tiles,), i32),
            pltpu.VMEM((16 * n_tiles + 24, BLK), F32),
            pltpu.VMEM((NQ // 2, n_tiles, 2 * BLK), BF16),
            pltpu.VMEM((n_yb * wx, BLK), F32),
            pltpu.VMEM((n_blk, 16, BLK), F32),
            pltpu.VMEM((n_blk, 16, BLK), BF16),
            pltpu.VMEM((n_blk, 16, BLK), BF16),
            pltpu.VMEM((2, n_yb, 16, BLK), BF16),
            pltpu.VMEM((2, n_yb, 16, BLK), BF16),
            pltpu.VMEM((2, NQ // 2 + 1, wx, BLK), BF16),
            pltpu.VMEM((2, NQ // 2 + 1, wx, BLK), BF16),
            pltpu.VMEM((128, BLK), F32),
            pltpu.VMEM((128, BLK), F32),
            dma((10,)), dma((4,)), dma((n_yb,)),
            dma((8,)), dma((8,)), dma((2,)), dma((2,)), dma((2,)), dma((2,)), dma((8,)), dma((8,)),
        ],
        compiler_params=pltpu.CompilerParams(
            collective_id=0, has_side_effects=True, vmem_limit_bytes=67043328 - 6291456 - 16384
        ),
    )(
        elem_volume.reshape(n_blk, BLK), elem_velocity, elem_energy.reshape(n_blk, BLK),
        elem_mat.reshape(n_blk, BLK), tile_cell.reshape(1, n_tiles),
        elem_dest, tile_slot, tile_cell, tile_count, mat_props,
        tile_weight, cell_state.reshape(NQ * wx, lanes),
    )
    out, pressure = pl.pallas_call(
        write_out,
        out_shape=(
            jax.ShapeDtypeStruct((NQ * wx, lanes), F32),
            jax.ShapeDtypeStruct((n_blk, BLK), BF16),
        ),
        in_specs=[vmem, vmem],
        out_specs=(hbm, vmem),
        scratch_shapes=[dma((8,))],
        compiler_params=pltpu.CompilerParams(vmem_limit_bytes=4 * 1024 * 1024),
    )(fresh, eo)
    return out.reshape(NQ, wx, lanes), pressure.reshape(n_blk * BLK)


def solution(mesh):
    both = ("gx", "gy")
    return jax.shard_map(
        per_device,
        mesh=mesh,
        in_specs=(
            P(both), P(None, both), P(both), P(both), P(both), P(both), P(both),
            P(both, None, None), P(both), P(None, "gx", "gy"), P(),
        ),
        out_specs=(P(None, "gx", "gy"), P(both)),
        check_vma=False,
    )
```
